32 devices in a mesh: groups: 2 (over y), blk: 4 (over z), head: 2 (over x), pair: 2 (over core).
Axes of the slice: x: 2, y: 2, z: 4, core: 2. Of those that a mesh axis runs over, the one named last changes fastest.
Arguments:
- single: bfloat16 [256, 384], P(('groups', 'blk')), parts along dimension 0, may hold values from -6 to 6
- pair: bfloat16 [256, 4, 32, 128], P(('groups', 'blk'), None, 'pair'), parts along dimension 0, may hold values from -6 to 6
- frames: float32 [12, 256], P(None, ('groups', 'blk')), parts along dimension 1, as said below
- chain: int32 [256], P(('groups', 'blk')), parts along dimension 0, may hold values from 0 to 5, never falling along the last dimension, each value on 1 to 42 neighbouring positions
- mask: int32 [256], P(('groups', 'blk')), parts along dimension 0, may hold values 0 or 1
- w_query: bfloat16 [384, 192], P(None, 'head'), may hold values from -0.3125 to 0.3125
- w_key_value: bfloat16 [384, 384], P(None, 'head'), may hold values from -0.3125 to 0.3125
- w_query_points: bfloat16 [384, 144], P(None, 'head'), may hold values from -0.3125 to 0.3125
- w_kv_points: bfloat16 [384, 432], P(None, 'head'), may hold values from -0.3125 to 0.3125
- w_pair_bias: bfloat16 [128, 12], P(None, 'head'), may hold values from -0.5 to 0.5
- head_weights: float32 [12], P('head'), may hold values from -9 to 1
- chain_bias: float32 [12], P('head'), may hold values from -3 to 3
- w_out: bfloat16 [12, 176, 384], P('head'), may hold values from -0.125 to 0.125
- out_gain: float32 [384], replicated, may hold values from 0.5 to 1.5
- w_backbone: bfloat16 [384, 6], replicated, may hold values from -0.3125 to 0.3125
Outputs:
- single_out: bfloat16 [256, 384], P(('groups', 'blk')), parts along dimension 0
- frames_out: float32 [12, 256], P(None, 'groups'), parts along dimension 1
The draws below stay inside these ranges and needn't reach their ends.
There are 2 independent parts, one for each index of `groups`. The reference program is written for one: setup_inputs(seed, part) draws one part's arguments, and reference() takes and returns one part's arrays. A program takes and returns all parts, laid end to end along the dimension named above; an argument that names none is the same for every part. Nothing has to cross between parts.
Inputs may be any that keep to these rules, and one draw needn't show every extreme that they name: `frames`: rows 0 to 8 of every column hold an orthonormal rotation matrix row by row; rows 9 to 11 the translation.
All inputs are finite; a program needn't handle non-finite values. No bound on the sum of `mask` on one device may be relied on, other than what follows from the above.
Results may differ from the reference program's by a relative error of at most 0.0048.
Values sent between devices are 32-bit elements; how exact they have to be, the bound alone decides.
A program may use at most 64 MiB of HBM per device.

```python
import math
import jax
import jax.numpy as jnp
import numpy as np
from jax import lax

C = 384
CZ = 128
HEADS = 12
CH = 16
PQ = 4
PV = 8
ROW_DEV = 32
N_RES = 128
KEY_BLOCKS = 4
CAT = 176
N_BLK = 4


def draw_frames(key, part):
    key_turn = jax.random.fold_in(key, 101)
    key_walk = jax.random.fold_in(key, 202)
    quaternion = jax.random.normal(key_turn, (4, N_RES), jnp.float32)
    quaternion = quaternion / jnp.sqrt(jnp.sum(quaternion * quaternion, axis=0, keepdims=True) + 1e-12)
    quat_a = quaternion[0]
    quat_b = quaternion[1]
    quat_c = quaternion[2]
    quat_d = quaternion[3]
    spin = jnp.stack([quat_a * quat_a + quat_b * quat_b - quat_c * quat_c - quat_d * quat_d, 2.0 * (quat_b * quat_c - quat_a * quat_d), 2.0 * (quat_b * quat_d + quat_a * quat_c), 2.0 * (quat_b * quat_c + quat_a * quat_d), quat_a * quat_a - quat_b * quat_b + quat_c * quat_c - quat_d * quat_d, 2.0 * (quat_c * quat_d - quat_a * quat_b), 2.0 * (quat_b * quat_d - quat_a * quat_c), 2.0 * (quat_c * quat_d + quat_a * quat_b), quat_a * quat_a - quat_b * quat_b - quat_c * quat_c + quat_d * quat_d])
    steps = jax.random.normal(key_walk, (3, N_RES), jnp.float32) * 2.2
    walk = jnp.cumsum(steps, axis=1)
    walk = walk - jnp.mean(walk, axis=1, keepdims=True)
    return jnp.concatenate([spin, walk], axis=0).astype(jnp.float32)


def plant(array, stream_key, smallest, high):
    longest = array.shape.index(max(array.shape))
    spots = []
    for shift in (0, 1):
        where = [jax.random.randint(jax.random.fold_in(stream_key, axis), (), 0, length) for axis, length in enumerate(array.shape)]
        where[longest] = (where[longest] + shift) % array.shape[longest]
        spots.append(tuple(where))
    return array.at[spots[0]].set(smallest).at[spots[1]].set(high)


def block_scale(own_key, dims, cuts, least, largest):
    loudness = 1.0
    for dim, blocks in cuts:
        draws = jax.random.uniform(jax.random.fold_in(jax.random.fold_in(own_key, 6), dim), (blocks,), jnp.float32, least / len(cuts), largest / len(cuts))
        loudness = loudness * jnp.repeat(jnp.exp(draws), dims[dim] // blocks).reshape((-1,) + (1,) * (len(dims) - 1 - dim))
    return loudness


def length_profile(number_of, total, limit, slope):
    weights = [(1 << 20) // math.isqrt(rank ** slope) + 1 for rank in range(2, number_of + 1)]
    rest, counts = total - limit - (number_of - 1), [1] * (number_of - 1)
    while rest > 0:
        candidates = [i for i in range(number_of - 1) if counts[i] < limit]
        mass, left = sum([weights[i] for i in candidates]), rest
        for i in candidates:
            addition = min(limit - counts[i], max(1, left * weights[i] // mass), rest)
            counts[i] = counts[i] + addition
            rest = rest - addition
    return np.array([limit] + counts)


def uneven_parts(stream_key, number_of, total, limit, slope):
    if number_of == 2:
        one = jax.random.randint(stream_key, (), max(1, total - limit), min(limit, total - 1) + 1)
        return jnp.stack([one, total - one])
    tallies = jnp.asarray(length_profile(number_of, total, limit, slope), jnp.int32)
    twos = (number_of - 1) // 2
    source_of, taker = tallies[1:1 + 2 * twos:2], tallies[2:2 + 2 * twos:2]
    slack = jnp.minimum(source_of - 1, limit - taker)
    moved = jax.random.randint(jax.random.fold_in(stream_key, 1), (twos,), 0, 1 << 20) % (slack + 1)
    tallies = tallies.at[1:1 + 2 * twos:2].set(source_of - moved).at[2:2 + 2 * twos:2].set(taker + moved)
    return tallies[jax.random.permutation(jax.random.fold_in(stream_key, 2), number_of)]


def scatter_about(own_key, extent, scale, bound, split=(), held_as=jnp.bfloat16):
    entries = scale * jax.random.normal(own_key, extent, jnp.float32)
    if split:
        entries = entries * block_scale(own_key, extent, split, -0.22, 0.18)
    return jnp.clip(entries, -bound, bound).astype(held_as)


def setup_inputs(seed: int = 0, part: int = 0) -> dict:
    arg_keys = jax.random.split(jax.random.key(seed), 16)
    part_keys = jax.random.split(jax.random.fold_in(arg_keys[15], part), 16)
    single = scatter_about(part_keys[0], (N_RES, C), 1.0, 6.0, ((0, 4),))
    pair = scatter_about(part_keys[1], (N_RES, KEY_BLOCKS, ROW_DEV, CZ), 1.0, 6.0, ((0, 4), (2, 2)))
    frames = draw_frames(jax.random.fold_in(jax.random.fold_in(arg_keys[15], part), 71), part)
    chain = jnp.searchsorted(jnp.cumsum(uneven_parts(part_keys[3], 6, N_RES, N_RES // 3, 0)), jnp.arange(N_RES), side="right").astype(jnp.int32)
    mask = plant((jax.random.randint(part_keys[4], (N_RES,), 0, 8) < 7).astype(jnp.int32), jax.random.fold_in(part_keys[4], 1), 0, 1)
    w_query = scatter_about(arg_keys[5], (C, HEADS * CH), C ** -0.5, 0.3125, ((1, 2),))
    w_key_value = scatter_about(arg_keys[6], (C, HEADS * 2 * CH), C ** -0.5, 0.3125, ((1, 2),))
    w_query_points = scatter_about(arg_keys[7], (C, HEADS * PQ * 3), C ** -0.5, 0.3125, ((1, 2),))
    w_kv_points = scatter_about(arg_keys[8], (C, HEADS * (PQ + PV) * 3), C ** -0.5, 0.3125, ((1, 2),))
    w_pair_bias = scatter_about(arg_keys[9], (CZ, HEADS), CZ ** -0.5, 0.5, ((1, 2),))
    head_weights = jnp.clip(-9.0 + 10.0 * jax.random.uniform(arg_keys[10], (HEADS,), jnp.float32) ** block_scale(arg_keys[10], (HEADS,), ((0, 2),), -0.2, 0.2), -9.0, 1.0)
    chain_bias = jnp.clip(jax.random.uniform(arg_keys[11], (HEADS,), jnp.float32, -3.0, 3.0) * block_scale(arg_keys[11], (HEADS,), ((0, 2),), -0.4, 0.0), -3.0, 3.0)
    w_out = scatter_about(arg_keys[12], (HEADS, CAT, C), (HEADS * CAT) ** -0.5, 0.125, ((0, 2),))
    out_gain = jnp.clip(1.0 + 0.1 * jax.random.normal(arg_keys[13], (C,), jnp.float32), 0.5, 1.5)
    w_backbone = scatter_about(arg_keys[14], (C, 6), C ** -0.5, 0.3125)
    return dict(single=single, pair=pair, frames=frames, chain=chain, mask=mask, w_query=w_query, w_key_value=w_key_value, w_query_points=w_query_points, w_kv_points=w_kv_points, w_pair_bias=w_pair_bias, head_weights=head_weights, chain_bias=chain_bias, w_out=w_out, out_gain=out_gain, w_backbone=w_backbone)


HIGH = lax.Precision.HIGHEST
LOGIT_WEIGHT = math.sqrt(1.0 / 3.0)
MASK_PENALTY = 100000.0

def to_global(local, frames):
    rotation = frames[:9].reshape(3, 3, -1)
    moved = jnp.einsum('abn,ngb->nga', rotation, local, precision=HIGH)
    return moved + jnp.transpose(frames[9:12])[:, None, :]

def to_local(points, frames):
    rotation = frames[:9].reshape(3, 3, -1)
    moved = points - jnp.transpose(frames[9:12])[:, None, None, :]
    return jnp.einsum('abn,nhpa->nhpb', rotation, moved, precision=HIGH)

def compose(frames, motion):
    rotation = frames[:9].reshape(3, 3, -1)
    inverse = 1.0 / jnp.sqrt(1.0 + motion[:, 0] ** 2 + motion[:, 1] ** 2 + motion[:, 2] ** 2)
    quat_a = inverse
    quat_b = motion[:, 0] * inverse
    quat_c = motion[:, 1] * inverse
    quat_d = motion[:, 2] * inverse
    spin = jnp.stack([quat_a * quat_a + quat_b * quat_b - quat_c * quat_c - quat_d * quat_d, 2.0 * (quat_b * quat_c - quat_a * quat_d), 2.0 * (quat_b * quat_d + quat_a * quat_c), 2.0 * (quat_b * quat_c + quat_a * quat_d), quat_a * quat_a - quat_b * quat_b + quat_c * quat_c - quat_d * quat_d, 2.0 * (quat_c * quat_d - quat_a * quat_b), 2.0 * (quat_b * quat_d - quat_a * quat_c), 2.0 * (quat_c * quat_d + quat_a * quat_b), quat_a * quat_a - quat_b * quat_b - quat_c * quat_c + quat_d * quat_d]).reshape(3, 3, -1)
    new_rotation = jnp.einsum('abn,bcn->acn', rotation, spin, precision=HIGH)
    offset = jnp.einsum('abn,nb->an', rotation, motion[:, 3:6], precision=HIGH)
    return jnp.concatenate([new_rotation.reshape(9, -1), frames[9:12] + offset], axis=0)

def attention_logits(pair_rows, query_rows, query_points, query_chain, query_present, keys, key_points, key_chain, key_present, w_pair_bias, distance_scale, chain_bias):
    count_q = pair_rows.shape[0]
    count_k = pair_rows.shape[1]
    bias = jnp.dot(pair_rows.reshape(count_q * count_k, -1), w_pair_bias, preferred_element_type=jnp.float32).reshape(count_q, count_k, -1)
    dots = jnp.einsum('ihc,jhc->ijh', query_rows, keys, precision=HIGH) / math.sqrt(keys.shape[-1])
    gaps = query_points[:, None] - key_points[None]
    distance = lax.optimization_barrier(jnp.sum(gaps * gaps, axis=(3, 4)))
    differ = (query_chain[:, None] != key_chain[None, :]).astype(jnp.float32)
    logits = LOGIT_WEIGHT * (dots + bias - distance_scale * distance + chain_bias * differ[..., None])
    absent = 1.0 - query_present[:, None] * key_present[None, :]
    return logits - MASK_PENALTY * absent[..., None]

def reference(single, pair, frames, chain, mask, w_query, w_key_value, w_query_points, w_kv_points, w_pair_bias, head_weights, chain_bias, w_out, out_gain, w_backbone):
    count = N_RES
    query = jnp.dot(single, w_query, preferred_element_type=jnp.float32).reshape(count, HEADS, CH)
    key_value = jnp.dot(single, w_key_value, preferred_element_type=jnp.float32).reshape(count, HEADS, 2, CH)
    keys = key_value[:, :, 0]
    values = key_value[:, :, 1]
    query_local = jnp.dot(single, w_query_points, preferred_element_type=jnp.float32).reshape(count, HEADS * PQ, 3)
    query_points = to_global(query_local, frames).reshape(count, HEADS, PQ, 3)
    pair_local = jnp.dot(single, w_kv_points, preferred_element_type=jnp.float32).reshape(count, HEADS * (PQ + PV), 3)
    point_pairs = to_global(pair_local, frames).reshape(count, HEADS, PQ + PV, 3)
    key_points = point_pairs[:, :, :PQ]
    value_points = point_pairs[:, :, PQ:]
    distance_scale = jax.nn.softplus(head_weights) * math.sqrt(2.0 / (9.0 * PQ)) / 2.0
    chain_float = chain.astype(jnp.float32)
    present = mask.astype(jnp.float32)
    pair_flat = pair.reshape(count, count, CZ)
    w_flat = w_out.reshape(HEADS * CAT, C)

    def block_rows(start):
        pair_rows = lax.dynamic_slice_in_dim(pair_flat, start, ROW_DEV, 0)
        query_rows = lax.dynamic_slice_in_dim(query, start, ROW_DEV, 0)
        qpoint_rows = lax.dynamic_slice_in_dim(query_points, start, ROW_DEV, 0)
        chain_rows = lax.dynamic_slice_in_dim(chain_float, start, ROW_DEV, 0)
        present_rows = lax.dynamic_slice_in_dim(present, start, ROW_DEV, 0)
        frame_rows = lax.dynamic_slice_in_dim(frames, start, ROW_DEV, 1)
        logits = attention_logits(pair_rows, query_rows, qpoint_rows, chain_rows, present_rows, keys, key_points, chain_float, present, w_pair_bias, distance_scale, chain_bias)
        top = lax.optimization_barrier(jnp.max(logits, axis=1))
        weights = jnp.exp(logits - top[:, None, :])
        total = lax.optimization_barrier(jnp.sum(weights, axis=1))
        attended = jnp.einsum('ijh,jhc->ihc', weights, values, precision=HIGH) / total[..., None]
        pointed_global = jnp.einsum('ijh,jhpd->ihpd', weights, value_points, precision=HIGH) / total[..., None, None]
        rounded = lax.optimization_barrier(weights.astype(jnp.bfloat16)).astype(jnp.float32)
        paired = jnp.einsum('ijh,ijc->ihc', rounded, pair_rows.astype(jnp.float32), precision=HIGH) / total[..., None]
        pointed = to_local(pointed_global, frame_rows)
        point_norms = jnp.sqrt(lax.optimization_barrier(jnp.sum(pointed * pointed, axis=3)) + 1.0)
        joined = jnp.concatenate([attended, pointed.reshape(ROW_DEV, HEADS, PV * 3), point_norms, paired], axis=2).astype(jnp.bfloat16)
        return jnp.dot(joined.reshape(ROW_DEV, HEADS * CAT), w_flat, preferred_element_type=jnp.float32)
    starts = jnp.arange(N_BLK, dtype=jnp.int32) * ROW_DEV
    update = lax.map(block_rows, starts).reshape(count, C)
    mixed = single.astype(jnp.float32) + update
    centre = lax.optimization_barrier(jnp.mean(mixed, axis=1, keepdims=True))
    spread = lax.optimization_barrier(jnp.mean(jnp.square(mixed - centre), axis=1, keepdims=True))
    single_out = ((mixed - centre) * lax.rsqrt(spread + 1e-05) * out_gain).astype(jnp.bfloat16)
    motion = jnp.dot(single_out, w_backbone, preferred_element_type=jnp.float32)
    frames_out = compose(frames, motion)
    return (single_out, frames_out)
```

```python
import functools
import math

import jax
import jax.numpy as jnp
import numpy as np
from jax import lax
from jax.experimental import pallas as pl
from jax.experimental.pallas import tpu as pltpu
from jax.sharding import PartitionSpec as P

LOGIT_WEIGHT = math.sqrt(1.0 / 3.0)
MASK_PENALTY = 100000.0
MESH = pl.DeviceIdType.MESH
LANES = 128
SUB = 8


def up(value, unit):
    return -(-value // unit) * unit


def nt(a, b):
    return lax.dot_general(a, b, (((1,), (1,)), ((), ())), preferred_element_type=jnp.float32)


def nn(a, b):
    return lax.dot_general(a, b, (((1,), (0,)), ((), ())), preferred_element_type=jnp.float32)


def halves(value):
    high = value.astype(jnp.bfloat16)
    return high, (value - high.astype(jnp.float32)).astype(jnp.bfloat16)


def dot3(product, a, b):
    a_high, a_low = halves(a)
    b_high, b_low = halves(b)
    return product(a_high, b_high) + (product(a_low, b_high) + product(a_high, b_low))


def selectors(heads, size, queries, values):
    wide = up(heads * max(size, values), LANES)
    sel_q = np.zeros((3 * queries * SUB, heads * queries * 3), np.float32)
    key_rows = up(heads * size, 16)
    sel_kv = np.zeros((key_rows + wide, heads * 2 * size), np.float32)
    sel_kp = np.zeros((3 * queries * SUB + 3 * wide, heads * (queries + values) * 3), np.float32)
    small = size + 4 * values
    sel_out = np.zeros((5 * wide, heads * small), np.float32)
    for h in range(heads):
        for b in range(3):
            for p in range(queries):
                row = (b * queries + p) * SUB + h
                sel_q[row, (h * queries + p) * 3 + b] = 1
                sel_kp[row, (h * (queries + values) + p) * 3 + b] = 1
            for p in range(values):
                row = 3 * queries * SUB + b * wide + h * values + p
                sel_kp[row, (h * (queries + values) + queries + p) * 3 + b] = 1
                sel_out[(1 + b) * wide + h * values + p, h * small + size + p * 3 + b] = 1
        for p in range(values):
            sel_out[4 * wide + h * values + p, h * small + size + 3 * values + p] = 1
        for c in range(size):
            sel_kv[h * size + c, h * 2 * size + c] = 1
            sel_kv[key_rows + h * size + c, h * 2 * size + size + c] = 1
            sel_out[h * size + c, h * small + c] = 1
    return [jnp.asarray(s, jnp.bfloat16) for s in (sel_q, sel_kv, sel_kp, sel_out)]


def kernel(
    dims,
    single_ref, pair_hbm, frames_ref, chain_row_ref, mask_row_ref, chain_ref, mask_ref,
    wq_ref, wkv_ref, wqp_ref, wkp_ref, wpb_ref, hw_ref, cb_ref, wout_hbm, gain_ref, wbb_ref,
    selq_ref, selkv_ref, selkp_ref, selout_ref,
    so_ref, fo_ref,
    gath, meta_s, pair_v, wout_v, sp, ex, red, fg,
    load_sem, gs_sem, gr_sem, es_sem, er_sem, rs_sem, rr_sem, fs_sem, fr_sem,
):
    nb, nh, npr, heads, size, queries, values = dims
    rows, width = single_ref.shape
    half = rows // npr
    keys = nb * half
    wide = up(heads * max(size, values), LANES)
    me_b = lax.axis_index("blk")
    me_h = lax.axis_index("head")
    me_p = lax.axis_index("pair")
    f32, bf16 = jnp.float32, jnp.bfloat16

    def blk_peer(d):
        return {"blk": lax.rem(me_b + d, nb)}

    def group_peer(dh, dp):
        return {"head": lax.rem(me_h + dh, nh), "pair": lax.rem(me_p + dp, npr)}

    group = [(dh, dp) for dh in range(nh) for dp in range(npr) if dh or dp]
    load_pair = pltpu.make_async_copy(pair_hbm, pair_v, load_sem.at[0])
    load_pair.start()
    load_out = pltpu.make_async_copy(wout_hbm, wout_v, load_sem.at[1])
    load_out.start()
    barrier = pltpu.get_barrier_semaphore()
    for d in range(1, nb):
        pl.semaphore_signal(barrier, inc=1, device_id=blk_peer(d), device_id_type=MESH)
    for dh, dp in group:
        pl.semaphore_signal(barrier, inc=1, device_id=group_peer(dh, dp), device_id_type=MESH)

    frames = frames_ref[...]
    meta = jnp.concatenate(
        [
            frames,
            chain_row_ref[...].astype(f32),
            mask_row_ref[...].astype(f32),
            jnp.zeros((LANES - 14, rows), f32),
        ],
        axis=0,
    ).T
    meta_s[...] = meta
    start = pl.multiple_of(me_p * half, half)
    gath[me_b, :, :width] = single_ref[pl.ds(start, half), :].astype(f32)
    gath[me_b, :, width:] = meta_s[pl.ds(start, half), :]

    single = single_ref[...]
    w_kv = nt(selkv_ref[...], wkv_ref[...]).astype(bf16)
    w_kp = nt(selkp_ref[...], wkp_ref[...]).astype(bf16)

    pl.semaphore_wait(barrier, nb - 1 + len(group))
    gathers = []
    for d in range(1, nb):
        copy = pltpu.make_async_remote_copy(
            src_ref=gath.at[me_b],
            dst_ref=gath.at[me_b],
            send_sem=gs_sem.at[d],
            recv_sem=gr_sem.at[d],
            device_id=blk_peer(d),
            device_id_type=MESH,
        )
        copy.start()
        gathers.append(copy)

    w_qp = nt(selq_ref[...], wqp_ref[...]).astype(bf16)
    query = nn(single, wq_ref[...]) * (1.0 / math.sqrt(size))
    q_local = nt(w_qp, single)
    step = queries * SUB

    def moved(local, base, count, turn):
        out = []
        for a in range(3):
            total = turn[9 + a : 10 + a]
            mixed = sum(
                turn[3 * a + b : 3 * a + b + 1] * local[base + b * count : base + (b + 1) * count]
                for b in range(3)
            )
            out.append(mixed + total)
        return out

    q_global = moved(q_local, 0, step, frames)
    eye = (
        lax.broadcasted_iota(jnp.int32, (SUB, heads), 0)
        == lax.broadcasted_iota(jnp.int32, (SUB, heads), 1)
    ).astype(bf16)
    w_bias = nt(eye, wpb_ref[...]).astype(bf16)
    eye6 = (
        lax.broadcasted_iota(jnp.int32, (SUB, wbb_ref.shape[1]), 0)
        == lax.broadcasted_iota(jnp.int32, (SUB, wbb_ref.shape[1]), 1)
    ).astype(bf16)
    w_back = nt(eye6, wbb_ref[...]).astype(bf16)
    head_row = lax.broadcasted_iota(jnp.int32, (SUB, keys), 0)
    raw = jnp.zeros((SUB, keys), f32)
    chain_term = jnp.zeros((SUB, keys), f32)
    for h in range(heads):
        raw = jnp.where(head_row == h, hw_ref[h], raw)
        chain_term = jnp.where(head_row == h, cb_ref[h], chain_term)
    soft = jnp.maximum(raw, 0.0) + jnp.log1p(jnp.exp(-jnp.abs(raw)))
    distance_scale = soft * (math.sqrt(2.0 / (9.0 * queries)) / 2.0)
    own_head = (
        lax.broadcasted_iota(jnp.int32, (SUB, heads * size), 1) // size
        == lax.broadcasted_iota(jnp.int32, (SUB, heads * size), 0)
    ).astype(f32)
    q_wide = (query[:, None, :] * own_head[None]).reshape(rows * SUB, heads * size)
    load_pair.wait()
    pairs = [pair_v[i * keys : (i + 1) * keys, :] for i in range(rows)]
    biases = [nt(w_bias, pairs[i]) for i in range(rows)]
    load_out.wait()
    small = size + 4 * values
    w_small = nn(
        selout_ref[...], jnp.concatenate([wout_v[h, :small, :] for h in range(heads)], axis=0)
    ).astype(bf16)

    for copy in gathers:
        copy.wait()
    everyone = gath[...].reshape(keys, width + LANES)
    key_single = everyone[:, :width].astype(bf16)
    key_meta = everyone[:, width:].T
    kv = nt(w_kv, key_single)
    key_rows = up(heads * size, 16)
    kp = nt(w_kp, key_single)
    k_global = moved(kp, 0, step, key_meta)
    v_global = moved(kp, 3 * step, wide, key_meta)
    dots = dot3(nn, q_wide, kv[: heads * size])
    key_chain = jnp.broadcast_to(key_meta[12:13], (SUB, keys))
    key_present = jnp.broadcast_to(key_meta[13:14], (SUB, keys))

    weights, tops, totals = [], [], []
    for i in range(rows):
        distance = jnp.zeros((SUB, keys), f32)
        for a in range(3):
            for p in range(queries):
                gap = (
                    q_global[a][p * SUB : (p + 1) * SUB, i : i + 1]
                    - k_global[a][p * SUB : (p + 1) * SUB, :]
                )
                distance = distance + gap * gap
        differ = jnp.where(key_chain != chain_ref[i].astype(f32), chain_term, 0.0)
        logits = LOGIT_WEIGHT * (
            dots[i * SUB : (i + 1) * SUB] + biases[i] - distance_scale * distance + differ
        )
        absent = 1.0 - mask_ref[i].astype(f32) * key_present
        logits = logits - MASK_PENALTY * absent
        top = jnp.max(logits, axis=1, keepdims=True)
        weight = jnp.exp(logits - top)
        weights.append(weight)
        tops.append(jnp.broadcast_to(top, (SUB, LANES)))
        totals.append(jnp.broadcast_to(jnp.sum(weight, axis=1, keepdims=True), (SUB, LANES)))

    lane = lax.broadcasted_iota(jnp.int32, (SUB, LANES), 1)
    row = lax.broadcasted_iota(jnp.int32, (SUB, LANES), 0)
    stat = jnp.concatenate(
        [
            jnp.sum(
                jnp.where(lane == row, tops[i], jnp.where(lane == row + SUB, totals[i], 0.0)),
                axis=0,
                keepdims=True,
            )
            for i in range(rows)
        ],
        axis=0,
    )
    wide_lane = lax.broadcasted_iota(jnp.int32, (SUB, wide), 1)
    wide_row = lax.broadcasted_iota(jnp.int32, (SUB, wide), 0)
    keep_value = (wide_lane // size == wide_row).astype(f32)
    keep_point = (wide_lane // values == wide_row).astype(f32)
    keep = jnp.concatenate([keep_value, keep_point, keep_point, keep_point], axis=1)
    every = jnp.concatenate(weights, axis=0)
    sums = dot3(nt, every, jnp.concatenate([kv[key_rows:]] + v_global, axis=0))
    sums = jnp.sum(sums.reshape(rows, SUB, 4 * wide) * keep[None], axis=1)
    ex[0, :, :LANES] = stat
    ex[0, :, LANES:] = sums[:, wide:]
    exchanges = []
    for d in range(1, npr):
        copy = pltpu.make_async_remote_copy(
            src_ref=ex.at[0],
            dst_ref=ex.at[d],
            send_sem=es_sem.at[d],
            recv_sem=er_sem.at[d],
            device_id=group_peer(0, d),
            device_id_type=MESH,
        )
        copy.start()
        exchanges.append(copy)

    for i in range(rows):
        sp[i * SUB : (i + 1) * SUB, :] = nn(weights[i].astype(bf16), pairs[i])

    for copy in exchanges:
        copy.wait()
    stats = [stat] + [ex[d, :, :LANES] for d in range(1, npr)]
    best = functools.reduce(jnp.maximum, [s[:, :SUB] for s in stats])
    scales = [jnp.exp(s[:, :SUB] - best) for s in stats]
    total = sum(s[:, SUB : 2 * SUB] * scale for s, scale in zip(stats, scales))
    factors = [scale / total for scale in scales]
    full_lane = lax.broadcasted_iota(jnp.int32, (rows, wide), 1)

    def spread(factor, count):
        out = jnp.zeros((rows, wide), f32)
        for h in range(heads):
            out = jnp.where(full_lane // count == h, factor[:, h : h + 1], out)
        return out

    attended = sums[:, :wide] * spread(factors[0], size)
    pointed_global = []
    for a in range(3):
        pointed_global.append(sums[:, (1 + a) * wide : (2 + a) * wide] * spread(factors[0], values))
    for d in range(1, npr):
        scale = spread(factors[d], values)
        for a in range(3):
            base = LANES + a * wide
            pointed_global[a] = pointed_global[a] + ex[d, :, base : base + wide] * scale
    shifted = [pointed_global[a] - meta[:, 9 + a : 10 + a] for a in range(3)]
    pointed = [
        sum(meta[:, 3 * a + b : 3 * a + b + 1] * shifted[a] for a in range(3)) for b in range(3)
    ]
    norms = jnp.sqrt(sum(p * p for p in pointed) + 1.0)
    features = [attended] + [p * (1.0 / npr) for p in pointed + [norms]]
    partial = sum(
        nn(feature.astype(bf16), w_small[k * wide : (k + 1) * wide])
        for k, feature in enumerate(features)
    )
    for h in range(heads):
        paired = sp[pl.ds(h, rows, stride=SUB), :] * factors[0][:, h : h + 1]
        partial = partial + nn(paired.astype(bf16), wout_v[h, small:, :])
    red[0] = partial
    reductions = []
    for dh, dp in group:
        code = dh * npr + dp
        copy = pltpu.make_async_remote_copy(
            src_ref=red.at[0],
            dst_ref=red.at[code],
            send_sem=rs_sem.at[code],
            recv_sem=rr_sem.at[code],
            device_id=group_peer(dh, dp),
            device_id_type=MESH,
        )
        copy.start()
        reductions.append(copy)
    for copy in reductions:
        copy.wait()
    update = jnp.zeros((rows, width), f32)
    for h in range(nh):
        for p in range(npr):
            code = lax.rem(me_h - h + nh, nh) * npr + lax.rem(me_p - p + npr, npr)
            update = update + red[code]
    mixed = single.astype(f32) + update
    centre = jnp.mean(mixed, axis=1, keepdims=True)
    away = mixed - centre
    variance = jnp.mean(away * away, axis=1, keepdims=True)
    out = (away * lax.rsqrt(variance + 1e-05) * gain_ref[...]).astype(bf16)
    so_ref[...] = out
    motion = nt(w_back, out)
    m = [motion[k : k + 1] for k in range(6)]
    inverse = 1.0 / jnp.sqrt(1.0 + m[0] * m[0] + m[1] * m[1] + m[2] * m[2])
    qa, qb, qc, qd = inverse, m[0] * inverse, m[1] * inverse, m[2] * inverse
    spin = [
        qa * qa + qb * qb - qc * qc - qd * qd,
        2.0 * (qb * qc - qa * qd),
        2.0 * (qb * qd + qa * qc),
        2.0 * (qb * qc + qa * qd),
        qa * qa - qb * qb + qc * qc - qd * qd,
        2.0 * (qc * qd - qa * qb),
        2.0 * (qb * qd - qa * qc),
        2.0 * (qc * qd + qa * qb),
        qa * qa - qb * qb - qc * qc + qd * qd,
    ]
    turn = [frames[k : k + 1] for k in range(12)]
    lines = [
        sum(turn[3 * a + b] * spin[3 * b + c] for b in range(3)) for a in range(3) for c in range(3)
    ]
    lines += [
        turn[9 + a] + sum(turn[3 * a + b] * m[3 + b] for b in range(3)) for a in range(3)
    ]
    fg[me_b] = jnp.concatenate(lines + [jnp.zeros((4, rows), f32)], axis=0)
    finals = []
    for d in range(1, nb):
        copy = pltpu.make_async_remote_copy(
            src_ref=fg.at[me_b],
            dst_ref=fg.at[me_b],
            send_sem=fs_sem.at[d],
            recv_sem=fr_sem.at[d],
            device_id=blk_peer(d),
            device_id_type=MESH,
        )
        copy.start()
        finals.append(copy)
    for copy in finals:
        copy.wait()
    for k in range(nb):
        fo_ref[:, k * rows : (k + 1) * rows] = fg[k, :12, :]


def body(
    single, pair, frames, chain, mask, w_query, w_key_value, w_query_points, w_kv_points,
    w_pair_bias, head_weights, chain_bias, w_out, out_gain, w_backbone,
):
    nb, nh, npr = (lax.axis_size(a) for a in ("blk", "head", "pair"))
    rows, width = single.shape
    half = rows // npr
    channels = pair.shape[3]
    heads = w_pair_bias.shape[1]
    size = w_query.shape[1] // heads
    queries = w_query_points.shape[1] // (3 * heads)
    values = w_kv_points.shape[1] // (3 * heads) - queries
    wide = up(heads * max(size, values), LANES)
    dims = (nb, nh, npr, heads, size, queries, values)
    vmem = pl.BlockSpec(memory_space=pltpu.VMEM)
    smem = pl.BlockSpec(memory_space=pltpu.SMEM)
    far = pl.BlockSpec(memory_space=pl.ANY)
    dma = pltpu.SemaphoreType.DMA
    flat = pair.reshape(rows * nb * half, channels)
    return tuple(
        pl.pallas_call(
            functools.partial(kernel, dims),
            out_shape=(
                jax.ShapeDtypeStruct((rows, width), jnp.bfloat16),
                jax.ShapeDtypeStruct((12, nb * rows), jnp.float32),
            ),
            in_specs=[
                vmem, far, vmem, vmem, vmem, smem, smem, vmem, vmem, vmem, vmem, vmem, smem, smem,
                far, vmem, vmem, vmem, vmem, vmem, vmem,
            ],
            out_specs=(vmem, vmem),
            scratch_shapes=[
                pltpu.VMEM((nb, half, width + LANES), jnp.float32),
                pltpu.VMEM((rows, LANES), jnp.float32),
                pltpu.VMEM(flat.shape, flat.dtype),
                pltpu.VMEM(w_out.shape, w_out.dtype),
                pltpu.VMEM((rows * SUB, channels), jnp.float32),
                pltpu.VMEM((npr, rows, LANES + 3 * wide), jnp.float32),
                pltpu.VMEM((nh * npr, rows, width), jnp.float32),
                pltpu.VMEM((nb, 16, rows), jnp.float32),
                dma((2,)),
                dma((nb,)),
                dma((nb,)),
                dma((npr,)),
                dma((npr,)),
                dma((nh * npr,)),
                dma((nh * npr,)),
                dma((nb,)),
                dma((nb,)),
            ],
            compiler_params=pltpu.CompilerParams(collective_id=0, has_side_effects=True),
        )(
            single, flat, frames, chain.reshape(1, rows), mask.reshape(1, rows), chain, mask,
            w_query, w_key_value, w_query_points, w_kv_points, w_pair_bias, head_weights,
            chain_bias, w_out, out_gain.reshape(1, width), w_backbone,
            *selectors(heads, size, queries, values),
        )
    )


def solution(mesh):
    placed = (
        P(("groups", "blk"), None),
        P(("groups", "blk"), None, "pair", None),
        P(None, ("groups", "blk")),
        P(("groups", "blk")),
        P(("groups", "blk")),
        P(None, "head"),
        P(None, "head"),
        P(None, "head"),
        P(None, "head"),
        P(None, "head"),
        P("head"),
        P("head"),
        P("head", None, None),
        P(),
        P(),
    )
    return jax.shard_map(
        body,
        mesh=mesh,
        in_specs=placed,
        out_specs=(P(("groups", "blk"), None), P(None, "groups")),
        check_vma=False,
    )
```

```python
import functools
import math

import jax
import jax.numpy as jnp
import numpy as np
from jax import lax
from jax.experimental import pallas as pl
from jax.experimental.pallas import tpu as pltpu
from jax.sharding import PartitionSpec as P

LOGIT_WEIGHT = math.sqrt(1.0 / 3.0)
MASK_PENALTY = 100000.0
MESH = pl.DeviceIdType.MESH
LANES = 128
SUB = 8


def up(value, unit):
    return -(-value // unit) * unit


def nt(a, b):
    return lax.dot_general(a, b, (((1,), (1,)), ((), ())), preferred_element_type=jnp.float32)


def nn(a, b):
    return lax.dot_general(a, b, (((1,), (0,)), ((), ())), preferred_element_type=jnp.float32)


def halves(value):
    high = value.astype(jnp.bfloat16)
    return high, (value - high.astype(jnp.float32)).astype(jnp.bfloat16)


def dot3(product, a, b):
    a_high, a_low = halves(a)
    b_high, b_low = halves(b)
    return product(a_high, b_high) + (product(a_low, b_high) + product(a_high, b_low))


def selectors(heads, size, queries, values):
    wide = up(heads * max(size, values), LANES)
    sel_q = np.zeros((3 * queries * SUB, heads * queries * 3), np.float32)
    key_rows = up(heads * size, 16)
    sel_kv = np.zeros((key_rows + wide, heads * 2 * size), np.float32)
    sel_kp = np.zeros((3 * queries * SUB + 3 * wide, heads * (queries + values) * 3), np.float32)
    small = size + 4 * values
    sel_out = np.zeros((5 * wide, heads * small), np.float32)
    for h in range(heads):
        for b in range(3):
            for p in range(queries):
                row = (b * queries + p) * SUB + h
                sel_q[row, (h * queries + p) * 3 + b] = 1
                sel_kp[row, (h * (queries + values) + p) * 3 + b] = 1
            for p in range(values):
                row = 3 * queries * SUB + b * wide + h * values + p
                sel_kp[row, (h * (queries + values) + queries + p) * 3 + b] = 1
                sel_out[(1 + b) * wide + h * values + p, h * small + size + p * 3 + b] = 1
        for p in range(values):
            sel_out[4 * wide + h * values + p, h * small + size + 3 * values + p] = 1
        for c in range(size):
            sel_kv[h * size + c, h * 2 * size + c] = 1
            sel_kv[key_rows + h * size + c, h * 2 * size + size + c] = 1
            sel_out[h * size + c, h * small + c] = 1
    return [jnp.asarray(s, jnp.bfloat16) for s in (sel_q, sel_kv, sel_kp, sel_out)]


def kernel(
    dims,
    single_ref, pair_hbm, frames_ref, chain_row_ref, mask_row_ref, chain_ref, mask_ref,
    wq_ref, wkv_ref, wqp_ref, wkp_ref, wpb_ref, hw_ref, cb_ref, wout_hbm, gain_ref, wbb_ref,
    selq_ref, selkv_ref, selkp_ref, selout_ref,
    so_ref, fo_ref,
    gath, meta_s, pair_v, wout_v, sp, ex, red, fg,
    load_sem, gs_sem, gr_sem, es_sem, er_sem, rs_sem, rr_sem, fs_sem, fr_sem,
):
    nb, nh, npr, heads, size, queries, values = dims
    rows, width = single_ref.shape
    half = rows // npr
    keys = nb * half
    wide = up(heads * max(size, values), LANES)
    me_b = lax.axis_index("blk")
    me_h = lax.axis_index("head")
    me_p = lax.axis_index("pair")
    f32, bf16 = jnp.float32, jnp.bfloat16

    def blk_peer(d):
        return {"blk": lax.rem(me_b + d, nb)}

    def group_peer(dh, dp):
        return {"head": lax.rem(me_h + dh, nh), "pair": lax.rem(me_p + dp, npr)}

    group = [(dh, dp) for dh in range(nh) for dp in range(npr) if dh or dp]
    load_pair = pltpu.make_async_copy(pair_hbm, pair_v, load_sem.at[0])
    load_pair.start()
    load_out = pltpu.make_async_copy(wout_hbm, wout_v, load_sem.at[1])
    load_out.start()
    barrier = pltpu.get_barrier_semaphore()
    for d in range(1, nb):
        pl.semaphore_signal(barrier, inc=1, device_id=blk_peer(d), device_id_type=MESH)
    for dh, dp in group:
        pl.semaphore_signal(barrier, inc=1, device_id=group_peer(dh, dp), device_id_type=MESH)

    frames = frames_ref[...]
    meta = jnp.concatenate(
        [
            frames,
            chain_row_ref[...].astype(f32),
            mask_row_ref[...].astype(f32),
            jnp.zeros((LANES - 14, rows), f32),
        ],
        axis=0,
    ).T
    meta_s[...] = meta
    start = pl.multiple_of(me_p * half, half)
    gath[me_b, :, :width] = single_ref[pl.ds(start, half), :].astype(f32)
    gath[me_b, :, width:] = meta_s[pl.ds(start, half), :]

    single = single_ref[...]
    w_kv = nn(selkv_ref[...], wkv_ref[...]).astype(bf16)
    w_kp = nn(selkp_ref[...], wkp_ref[...]).astype(bf16)

    pl.semaphore_wait(barrier, nb - 1 + len(group))
    gathers = []
    for d in range(1, nb):
        copy = pltpu.make_async_remote_copy(
            src_ref=gath.at[me_b],
            dst_ref=gath.at[me_b],
            send_sem=gs_sem.at[d],
            recv_sem=gr_sem.at[d],
            device_id=blk_peer(d),
            device_id_type=MESH,
        )
        copy.start()
        gathers.append(copy)

    w_qp = nn(selq_ref[...], wqp_ref[...]).astype(bf16)
    query = nt(single, wq_ref[...]) * (1.0 / math.sqrt(size))
    q_local = nt(w_qp, single)
    step = queries * SUB

    def moved(local, base, count, turn):
        out = []
        for a in range(3):
            total = turn[9 + a : 10 + a]
            mixed = sum(
                turn[3 * a + b : 3 * a + b + 1] * local[base + b * count : base + (b + 1) * count]
                for b in range(3)
            )
            out.append(mixed + total)
        return out

    q_global = moved(q_local, 0, step, frames)
    eye = (
        lax.broadcasted_iota(jnp.int32, (SUB, heads), 0)
        == lax.broadcasted_iota(jnp.int32, (SUB, heads), 1)
    ).astype(bf16)
    w_bias = nn(eye, wpb_ref[...]).astype(bf16)
    eye6 = (
        lax.broadcasted_iota(jnp.int32, (SUB, wbb_ref.shape[0]), 0)
        == lax.broadcasted_iota(jnp.int32, (SUB, wbb_ref.shape[0]), 1)
    ).astype(bf16)
    w_back = nn(eye6, wbb_ref[...]).astype(bf16)
    head_row = lax.broadcasted_iota(jnp.int32, (SUB, keys), 0)
    raw = jnp.zeros((SUB, keys), f32)
    chain_term = jnp.zeros((SUB, keys), f32)
    for h in range(heads):
        raw = jnp.where(head_row == h, hw_ref[h], raw)
        chain_term = jnp.where(head_row == h, cb_ref[h], chain_term)
    soft = jnp.maximum(raw, 0.0) + jnp.log1p(jnp.exp(-jnp.abs(raw)))
    distance_scale = soft * (math.sqrt(2.0 / (9.0 * queries)) / 2.0)
    own_head = (
        lax.broadcasted_iota(jnp.int32, (SUB, heads * size), 1) // size
        == lax.broadcasted_iota(jnp.int32, (SUB, heads * size), 0)
    ).astype(f32)
    q_wide = (query[:, None, :] * own_head[None]).reshape(rows * SUB, heads * size)
    load_pair.wait()
    pairs = [pair_v[i * keys : (i + 1) * keys, :] for i in range(rows)]
    biases = [nt(w_bias, pairs[i]) for i in range(rows)]
    load_out.wait()
    small = size + 4 * values
    w_small = nn(
        selout_ref[...], jnp.concatenate([wout_v[h, :small, :] for h in range(heads)], axis=0)
    ).astype(bf16)

    for copy in gathers:
        copy.wait()
    everyone = gath[...].reshape(keys, width + LANES)
    key_single = everyone[:, :width].astype(bf16)
    key_meta = everyone[:, width:].T
    kv = nt(w_kv, key_single)
    key_rows = up(heads * size, 16)
    kp = nt(w_kp, key_single)
    k_global = moved(kp, 0, step, key_meta)
    v_global = moved(kp, 3 * step, wide, key_meta)
    dots = dot3(nn, q_wide, kv[: heads * size])
    key_chain = jnp.broadcast_to(key_meta[12:13], (SUB, keys))
    key_present = jnp.broadcast_to(key_meta[13:14], (SUB, keys))

    weights, tops, totals = [], [], []
    for i in range(rows):
        distance = jnp.zeros((SUB, keys), f32)
        for a in range(3):
            for p in range(queries):
                gap = (
                    q_global[a][p * SUB : (p + 1) * SUB, i : i + 1]
                    - k_global[a][p * SUB : (p + 1) * SUB, :]
                )
                distance = distance + gap * gap
        differ = jnp.where(key_chain != chain_ref[i].astype(f32), chain_term, 0.0)
        logits = LOGIT_WEIGHT * (
            dots[i * SUB : (i + 1) * SUB] + biases[i] - distance_scale * distance + differ
        )
        absent = 1.0 - mask_ref[i].astype(f32) * key_present
        logits = logits - MASK_PENALTY * absent
        top = jnp.max(logits, axis=1, keepdims=True)
        weight = jnp.exp(logits - top)
        weights.append(weight)
        tops.append(jnp.broadcast_to(top, (SUB, LANES)))
        totals.append(jnp.broadcast_to(jnp.sum(weight, axis=1, keepdims=True), (SUB, LANES)))

    lane = lax.broadcasted_iota(jnp.int32, (SUB, LANES), 1)
    row = lax.broadcasted_iota(jnp.int32, (SUB, LANES), 0)
    stat = jnp.concatenate(
        [
            jnp.sum(
                jnp.where(lane == row, tops[i], jnp.where(lane == row + SUB, totals[i], 0.0)),
                axis=0,
                keepdims=True,
            )
            for i in range(rows)
        ],
        axis=0,
    )
    wide_lane = lax.broadcasted_iota(jnp.int32, (SUB, wide), 1)
    wide_row = lax.broadcasted_iota(jnp.int32, (SUB, wide), 0)
    keep_value = (wide_lane // size == wide_row).astype(f32)
    keep_point = (wide_lane // values == wide_row).astype(f32)
    keep = jnp.concatenate([keep_value, keep_point, keep_point, keep_point], axis=1)
    every = jnp.concatenate(weights, axis=0)
    sums = dot3(nt, every, jnp.concatenate([kv[key_rows:]] + v_global, axis=0))
    sums = jnp.sum(sums.reshape(rows, SUB, 4 * wide) * keep[None], axis=1)
    ex[0, :, :LANES] = stat
    ex[0, :, LANES:] = sums[:, wide:]
    exchanges = []
    for d in range(1, npr):
        copy = pltpu.make_async_remote_copy(
            src_ref=ex.at[0],
            dst_ref=ex.at[d],
            send_sem=es_sem.at[d],
            recv_sem=er_sem.at[d],
            device_id=group_peer(0, d),
            device_id_type=MESH,
        )
        copy.start()
        exchanges.append(copy)

    for i in range(rows):
        sp[i * SUB : (i + 1) * SUB, :] = nn(weights[i].astype(bf16), pairs[i])

    for copy in exchanges:
        copy.wait()
    stats = [stat] + [ex[d, :, :LANES] for d in range(1, npr)]
    best = functools.reduce(jnp.maximum, [s[:, :SUB] for s in stats])
    scales = [jnp.exp(s[:, :SUB] - best) for s in stats]
    total = sum(s[:, SUB : 2 * SUB] * scale for s, scale in zip(stats, scales))
    factors = [scale / total for scale in scales]
    full_lane = lax.broadcasted_iota(jnp.int32, (rows, wide), 1)

    def spread(factor, count):
        out = jnp.zeros((rows, wide), f32)
        for h in range(heads):
            out = jnp.where(full_lane // count == h, factor[:, h : h + 1], out)
        return out

    attended = sums[:, :wide] * spread(factors[0], size)
    pointed_global = []
    for a in range(3):
        pointed_global.append(sums[:, (1 + a) * wide : (2 + a) * wide] * spread(factors[0], values))
    for d in range(1, npr):
        scale = spread(factors[d], values)
        for a in range(3):
            base = LANES + a * wide
            pointed_global[a] = pointed_global[a] + ex[d, :, base : base + wide] * scale
    shifted = [pointed_global[a] - meta[:, 9 + a : 10 + a] for a in range(3)]
    pointed = [
        sum(meta[:, 3 * a + b : 3 * a + b + 1] * shifted[a] for a in range(3)) for b in range(3)
    ]
    norms = jnp.sqrt(sum(p * p for p in pointed) + 1.0)
    features = [attended] + [p * (1.0 / npr) for p in pointed + [norms]]
    partial = sum(
        nn(feature.astype(bf16), w_small[k * wide : (k + 1) * wide])
        for k, feature in enumerate(features)
    )
    for h in range(heads):
        paired = sp[pl.ds(h, rows, stride=SUB), :] * factors[0][:, h : h + 1]
        partial = partial + nn(paired.astype(bf16), wout_v[h, small:, :])
    red[0] = partial
    reductions = []
    for dh, dp in group:
        code = dh * npr + dp
        copy = pltpu.make_async_remote_copy(
            src_ref=red.at[0],
            dst_ref=red.at[code],
            send_sem=rs_sem.at[code],
            recv_sem=rr_sem.at[code],
            device_id=group_peer(dh, dp),
            device_id_type=MESH,
        )
        copy.start()
        reductions.append(copy)
    for copy in reductions:
        copy.wait()
    update = jnp.zeros((rows, width), f32)
    for h in range(nh):
        for p in range(npr):
            code = lax.rem(me_h - h + nh, nh) * npr + lax.rem(me_p - p + npr, npr)
            update = update + red[code]
    mixed = single.astype(f32) + update
    centre = jnp.mean(mixed, axis=1, keepdims=True)
    away = mixed - centre
    variance = jnp.mean(away * away, axis=1, keepdims=True)
    out = (away * lax.rsqrt(variance + 1e-05) * gain_ref[...].reshape(1, width)).astype(bf16)
    so_ref[...] = out
    motion = nt(w_back, out)
    m = [motion[k : k + 1] for k in range(6)]
    inverse = 1.0 / jnp.sqrt(1.0 + m[0] * m[0] + m[1] * m[1] + m[2] * m[2])
    qa, qb, qc, qd = inverse, m[0] * inverse, m[1] * inverse, m[2] * inverse
    spin = [
        qa * qa + qb * qb - qc * qc - qd * qd,
        2.0 * (qb * qc - qa * qd),
        2.0 * (qb * qd + qa * qc),
        2.0 * (qb * qc + qa * qd),
        qa * qa - qb * qb + qc * qc - qd * qd,
        2.0 * (qc * qd - qa * qb),
        2.0 * (qb * qd - qa * qc),
        2.0 * (qc * qd + qa * qb),
        qa * qa - qb * qb - qc * qc + qd * qd,
    ]
    turn = [frames[k : k + 1] for k in range(12)]
    lines = [
        sum(turn[3 * a + b] * spin[3 * b + c] for b in range(3)) for a in range(3) for c in range(3)
    ]
    lines += [
        turn[9 + a] + sum(turn[3 * a + b] * m[3 + b] for b in range(3)) for a in range(3)
    ]
    fg[me_b] = jnp.concatenate(lines + [jnp.zeros((4, rows), f32)], axis=0)
    finals = []
    for d in range(1, nb):
        copy = pltpu.make_async_remote_copy(
            src_ref=fg.at[me_b],
            dst_ref=fg.at[me_b],
            send_sem=fs_sem.at[d],
            recv_sem=fr_sem.at[d],
            device_id=blk_peer(d),
            device_id_type=MESH,
        )
        copy.start()
        finals.append(copy)
    for copy in finals:
        copy.wait()
    for k in range(nb):
        fo_ref[:, k * rows : (k + 1) * rows] = fg[k, :12, :]


def body(
    single, pair, frames, chain, mask, w_query, w_key_value, w_query_points, w_kv_points,
    w_pair_bias, head_weights, chain_bias, w_out, out_gain, w_backbone,
):
    nb, nh, npr = (lax.axis_size(a) for a in ("blk", "head", "pair"))
    rows, width = single.shape
    half = rows // npr
    channels = pair.shape[3]
    heads = w_pair_bias.shape[1]
    size = w_query.shape[1] // heads
    queries = w_query_points.shape[1] // (3 * heads)
    values = w_kv_points.shape[1] // (3 * heads) - queries
    wide = up(heads * max(size, values), LANES)
    dims = (nb, nh, npr, heads, size, queries, values)
    vmem = pl.BlockSpec(memory_space=pltpu.VMEM)
    smem = pl.BlockSpec(memory_space=pltpu.SMEM)
    far = pl.BlockSpec(memory_space=pl.ANY)
    dma = pltpu.SemaphoreType.DMA
    flat = pair.reshape(rows * nb * half, channels)
    return tuple(
        pl.pallas_call(
            functools.partial(kernel, dims),
            out_shape=(
                jax.ShapeDtypeStruct((rows, width), jnp.bfloat16),
                jax.ShapeDtypeStruct((12, nb * rows), jnp.float32),
            ),
            in_specs=[
                vmem, far, vmem, vmem, vmem, smem, smem, vmem, vmem, vmem, vmem, vmem, smem, smem,
                far, vmem, vmem, vmem, vmem, vmem, vmem,
            ],
            out_specs=(vmem, vmem),
            scratch_shapes=[
                pltpu.VMEM((nb, half, width + LANES), jnp.float32),
                pltpu.VMEM((rows, LANES), jnp.float32),
                pltpu.VMEM(flat.shape, flat.dtype),
                pltpu.VMEM(w_out.shape, w_out.dtype),
                pltpu.VMEM((rows * SUB, channels), jnp.float32),
                pltpu.VMEM((npr, rows, LANES + 3 * wide), jnp.float32),
                pltpu.VMEM((nh * npr, rows, width), jnp.float32),
                pltpu.VMEM((nb, 16, rows), jnp.float32),
                dma((2,)),
                dma((nb,)),
                dma((nb,)),
                dma((npr,)),
                dma((npr,)),
                dma((nh * npr,)),
                dma((nh * npr,)),
                dma((nb,)),
                dma((nb,)),
            ],
            compiler_params=pltpu.CompilerParams(collective_id=0, has_side_effects=True),
        )(
            single, flat, frames, chain.reshape(1, rows), mask.reshape(1, rows), chain, mask,
            w_query.T, w_key_value.T, w_query_points.T, w_kv_points.T, w_pair_bias.T, head_weights,
            chain_bias, w_out, out_gain, w_backbone.T,
            *selectors(heads, size, queries, values),
        )
    )


def solution(mesh):
    placed = (
        P(("groups", "blk"), None),
        P(("groups", "blk"), None, "pair", None),
        P(None, ("groups", "blk")),
        P(("groups", "blk")),
        P(("groups", "blk")),
        P(None, "head"),
        P(None, "head"),
        P(None, "head"),
        P(None, "head"),
        P(None, "head"),
        P("head"),
        P("head"),
        P("head", None, None),
        P(),
        P(),
    )
    return jax.shard_map(
        body,
        mesh=mesh,
        in_specs=placed,
        out_specs=(P(("groups", "blk"), None), P(None, "groups")),
        check_vma=False,
    )
```

```python
import functools
import math

import jax
import jax.numpy as jnp
import numpy as np
from jax import lax
from jax.experimental import pallas as pl
from jax.experimental.pallas import tpu as pltpu
from jax.sharding import PartitionSpec as P

LOGIT_WEIGHT = math.sqrt(1.0 / 3.0)
MASK_PENALTY = 100000.0
MESH = pl.DeviceIdType.MESH
LANES = 128
SUB = 8


def up(value, unit):
    return -(-value // unit) * unit


def nt(a, b):
    return lax.dot_general(a, b, (((1,), (1,)), ((), ())), preferred_element_type=jnp.float32)


def nn(a, b):
    return lax.dot_general(a, b, (((1,), (0,)), ((), ())), preferred_element_type=jnp.float32)


def halves(value):
    high = value.astype(jnp.bfloat16)
    return high, (value - high.astype(jnp.float32)).astype(jnp.bfloat16)


def dot3(product, a, b):
    a_high, a_low = halves(a)
    b_high, b_low = halves(b)
    return product(a_high, b_high) + (product(a_low, b_high) + product(a_high, b_low))


def selectors(heads, size, queries, values):
    wide = up(heads * max(size, values), LANES)
    sel_q = np.zeros((3 * queries * SUB, heads * queries * 3), np.float32)
    key_rows = up(heads * size, 16)
    sel_kv = np.zeros((key_rows + wide, heads * 2 * size), np.float32)
    sel_kp = np.zeros((3 * queries * SUB + 3 * wide, heads * (queries + values) * 3), np.float32)
    small = size + 4 * values
    sel_out = np.zeros((5 * wide, heads * small), np.float32)
    for h in range(heads):
        for b in range(3):
            for p in range(queries):
                row = (b * queries + p) * SUB + h
                sel_q[row, (h * queries + p) * 3 + b] = 1
                sel_kp[row, (h * (queries + values) + p) * 3 + b] = 1
            for p in range(values):
                row = 3 * queries * SUB + b * wide + h * values + p
                sel_kp[row, (h * (queries + values) + queries + p) * 3 + b] = 1
                sel_out[(1 + b) * wide + h * values + p, h * small + size + p * 3 + b] = 1
        for p in range(values):
            sel_out[4 * wide + h * values + p, h * small + size + 3 * values + p] = 1
        for c in range(size):
            sel_kv[h * size + c, h * 2 * size + c] = 1
            sel_kv[key_rows + h * size + c, h * 2 * size + size + c] = 1
            sel_out[h * size + c, h * small + c] = 1
    return [jnp.asarray(s, jnp.bfloat16) for s in (sel_q, sel_kv, sel_kp, sel_out)]


ORDER = (
    "frames", "chain_row", "mask_row", "single", "sel_kv", "w_kv", "sel_kp", "w_kp", "sel_q", "w_qp",
    "w_q", "w_bias", "w_back", "head_weights", "chain_bias", "pair", "w_out", "sel_out", "chain",
    "mask", "gain",
)
SCALARS = ("head_weights", "chain_bias", "chain", "mask")


def kernel(dims, *refs):
    count = len(ORDER)
    far = refs[:count]
    so_ref, fo_ref = refs[count : count + 2]
    near = dict(zip(ORDER, refs[count + 2 : 2 * count + 2]))
    (
        gath, meta_s, sp, ex, red, fg,
        load_sem, gs_sem, gr_sem, es_sem, er_sem, rs_sem, rr_sem, fs_sem, fr_sem,
    ) = refs[2 * count + 2 :]
    loads = {
        name: pltpu.make_async_copy(source, near[name], load_sem.at[k])
        for k, (name, source) in enumerate(zip(ORDER, far))
    }
    for name in ORDER:
        loads[name].start()

    def loaded(name):
        loads[name].wait()
        return near[name]

    nb, nh, npr, heads, size, queries, values = dims
    rows, width = near["single"].shape
    half = rows // npr
    keys = nb * half
    wide = up(heads * max(size, values), LANES)
    me_b = lax.axis_index("blk")
    me_h = lax.axis_index("head")
    me_p = lax.axis_index("pair")
    f32, bf16 = jnp.float32, jnp.bfloat16

    def blk_peer(d):
        return {"blk": lax.rem(me_b + d, nb)}

    def group_peer(dh, dp):
        return {"head": lax.rem(me_h + dh, nh), "pair": lax.rem(me_p + dp, npr)}

    group = [(dh, dp) for dh in range(nh) for dp in range(npr) if dh or dp]
    barrier = pltpu.get_barrier_semaphore()
    for d in range(1, nb):
        pl.semaphore_signal(barrier, inc=1, device_id=blk_peer(d), device_id_type=MESH)
    for dh, dp in group:
        pl.semaphore_signal(barrier, inc=1, device_id=group_peer(dh, dp), device_id_type=MESH)

    frames = loaded("frames")[...]
    chain_row = loaded("chain_row")[...].astype(f32)
    mask_row = loaded("mask_row")[...].astype(f32)
    single_ref = loaded("single")
    meta = jnp.concatenate(
        [
            frames,
            chain_row,
            mask_row,
            jnp.zeros((LANES - 14, rows), f32),
        ],
        axis=0,
    ).T
    meta_s[...] = meta
    start = pl.multiple_of(me_p * half, half)
    gath[me_b, :, :width] = single_ref[pl.ds(start, half), :].astype(f32)
    gath[me_b, :, width:] = meta_s[pl.ds(start, half), :]

    single = single_ref[...]
    pl.semaphore_wait(barrier, nb - 1 + len(group))
    gathers = []
    for d in range(1, nb):
        copy = pltpu.make_async_remote_copy(
            src_ref=gath.at[me_b],
            dst_ref=gath.at[me_b],
            send_sem=gs_sem.at[d],
            recv_sem=gr_sem.at[d],
            device_id=blk_peer(d),
            device_id_type=MESH,
        )
        copy.start()
        gathers.append(copy)

    w_kv = nn(loaded("sel_kv")[...], loaded("w_kv")[...]).astype(bf16)
    w_kp = nn(loaded("sel_kp")[...], loaded("w_kp")[...]).astype(bf16)
    w_qp = nn(loaded("sel_q")[...], loaded("w_qp")[...]).astype(bf16)
    query = nt(single, loaded("w_q")[...]) * (1.0 / math.sqrt(size))
    q_local = nt(w_qp, single)
    step = queries * SUB

    def moved(local, base, count, turn):
        out = []
        for a in range(3):
            total = turn[9 + a : 10 + a]
            mixed = sum(
                turn[3 * a + b : 3 * a + b + 1] * local[base + b * count : base + (b + 1) * count]
                for b in range(3)
            )
            out.append(mixed + total)
        return out

    q_global = moved(q_local, 0, step, frames)
    eye = (
        lax.broadcasted_iota(jnp.int32, (SUB, heads), 0)
        == lax.broadcasted_iota(jnp.int32, (SUB, heads), 1)
    ).astype(bf16)
    w_bias = nn(eye, loaded("w_bias")[...]).astype(bf16)
    wbb_ref = loaded("w_back")
    eye6 = (
        lax.broadcasted_iota(jnp.int32, (SUB, wbb_ref.shape[0]), 0)
        == lax.broadcasted_iota(jnp.int32, (SUB, wbb_ref.shape[0]), 1)
    ).astype(bf16)
    w_back = nn(eye6, wbb_ref[...]).astype(bf16)
    head_row = lax.broadcasted_iota(jnp.int32, (SUB, keys), 0)
    raw = jnp.zeros((SUB, keys), f32)
    chain_term = jnp.zeros((SUB, keys), f32)
    hw_ref, cb_ref = loaded("head_weights"), loaded("chain_bias")
    for h in range(heads):
        raw = jnp.where(head_row == h, hw_ref[h], raw)
        chain_term = jnp.where(head_row == h, cb_ref[h], chain_term)
    soft = jnp.maximum(raw, 0.0) + jnp.log1p(jnp.exp(-jnp.abs(raw)))
    distance_scale = soft * (math.sqrt(2.0 / (9.0 * queries)) / 2.0)
    own_head = (
        lax.broadcasted_iota(jnp.int32, (SUB, heads * size), 1) // size
        == lax.broadcasted_iota(jnp.int32, (SUB, heads * size), 0)
    ).astype(f32)
    q_wide = (query[:, None, :] * own_head[None]).reshape(rows * SUB, heads * size)
    pair_v = loaded("pair")
    pairs = [pair_v[i * keys : (i + 1) * keys, :] for i in range(rows)]
    biases = [nt(w_bias, pairs[i]) for i in range(rows)]
    wout_v = loaded("w_out")
    small = size + 4 * values
    w_small = nn(
        loaded("sel_out")[...], jnp.concatenate([wout_v[h, :small, :] for h in range(heads)], axis=0)
    ).astype(bf16)

    for copy in gathers:
        copy.wait()
    everyone = gath[...].reshape(keys, width + LANES)
    key_single = everyone[:, :width].astype(bf16)
    key_meta = everyone[:, width:].T
    kv = nt(w_kv, key_single)
    key_rows = up(heads * size, 16)
    kp = nt(w_kp, key_single)
    k_global = moved(kp, 0, step, key_meta)
    v_global = moved(kp, 3 * step, wide, key_meta)
    dots = dot3(nn, q_wide, kv[: heads * size])
    key_chain = jnp.broadcast_to(key_meta[12:13], (SUB, keys))
    key_present = jnp.broadcast_to(key_meta[13:14], (SUB, keys))
    chain_ref, mask_ref = loaded("chain"), loaded("mask")

    weights, tops, totals = [], [], []
    for i in range(rows):
        distance = jnp.zeros((SUB, keys), f32)
        for a in range(3):
            for p in range(queries):
                gap = (
                    q_global[a][p * SUB : (p + 1) * SUB, i : i + 1]
                    - k_global[a][p * SUB : (p + 1) * SUB, :]
                )
                distance = distance + gap * gap
        differ = jnp.where(key_chain != chain_ref[i].astype(f32), chain_term, 0.0)
        logits = LOGIT_WEIGHT * (
            dots[i * SUB : (i + 1) * SUB] + biases[i] - distance_scale * distance + differ
        )
        absent = 1.0 - mask_ref[i].astype(f32) * key_present
        logits = logits - MASK_PENALTY * absent
        top = jnp.max(logits, axis=1, keepdims=True)
        weight = jnp.exp(logits - top)
        weights.append(weight)
        tops.append(jnp.broadcast_to(top, (SUB, LANES)))
        totals.append(jnp.broadcast_to(jnp.sum(weight, axis=1, keepdims=True), (SUB, LANES)))

    lane = lax.broadcasted_iota(jnp.int32, (SUB, LANES), 1)
    row = lax.broadcasted_iota(jnp.int32, (SUB, LANES), 0)
    stat = jnp.concatenate(
        [
            jnp.sum(
                jnp.where(lane == row, tops[i], jnp.where(lane == row + SUB, totals[i], 0.0)),
                axis=0,
                keepdims=True,
            )
            for i in range(rows)
        ],
        axis=0,
    )
    wide_lane = lax.broadcasted_iota(jnp.int32, (SUB, wide), 1)
    wide_row = lax.broadcasted_iota(jnp.int32, (SUB, wide), 0)
    keep_value = (wide_lane // size == wide_row).astype(f32)
    keep_point = (wide_lane // values == wide_row).astype(f32)
    keep = jnp.concatenate([keep_value, keep_point, keep_point, keep_point], axis=1)
    every = jnp.concatenate(weights, axis=0)
    sums = dot3(nt, every, jnp.concatenate([kv[key_rows:]] + v_global, axis=0))
    sums = jnp.sum(sums.reshape(rows, SUB, 4 * wide) * keep[None], axis=1)
    ex[0, :, :LANES] = stat
    ex[0, :, LANES:] = sums[:, wide:]
    exchanges = []
    for d in range(1, npr):
        copy = pltpu.make_async_remote_copy(
            src_ref=ex.at[0],
            dst_ref=ex.at[d],
            send_sem=es_sem.at[d],
            recv_sem=er_sem.at[d],
            device_id=group_peer(0, d),
            device_id_type=MESH,
        )
        copy.start()
        exchanges.append(copy)

    for i in range(rows):
        sp[i * SUB : (i + 1) * SUB, :] = nn(weights[i].astype(bf16), pairs[i])

    for copy in exchanges:
        copy.wait()
    stats = [stat] + [ex[d, :, :LANES] for d in range(1, npr)]
    best = functools.reduce(jnp.maximum, [s[:, :SUB] for s in stats])
    scales = [jnp.exp(s[:, :SUB] - best) for s in stats]
    total = sum(s[:, SUB : 2 * SUB] * scale for s, scale in zip(stats, scales))
    factors = [scale / total for scale in scales]
    full_lane = lax.broadcasted_iota(jnp.int32, (rows, wide), 1)

    def spread(factor, count):
        out = jnp.zeros((rows, wide), f32)
        for h in range(heads):
            out = jnp.where(full_lane // count == h, factor[:, h : h + 1], out)
        return out

    attended = sums[:, :wide] * spread(factors[0], size)
    pointed_global = []
    for a in range(3):
        pointed_global.append(sums[:, (1 + a) * wide : (2 + a) * wide] * spread(factors[0], values))
    for d in range(1, npr):
        scale = spread(factors[d], values)
        for a in range(3):
            base = LANES + a * wide
            pointed_global[a] = pointed_global[a] + ex[d, :, base : base + wide] * scale
    shifted = [pointed_global[a] - meta[:, 9 + a : 10 + a] for a in range(3)]
    pointed = [
        sum(meta[:, 3 * a + b : 3 * a + b + 1] * shifted[a] for a in range(3)) for b in range(3)
    ]
    norms = jnp.sqrt(sum(p * p for p in pointed) + 1.0)
    features = [attended] + [p * (1.0 / npr) for p in pointed + [norms]]
    partial = sum(
        nn(feature.astype(bf16), w_small[k * wide : (k + 1) * wide])
        for k, feature in enumerate(features)
    )
    for h in range(heads):
        paired = sp[pl.ds(h, rows, stride=SUB), :] * factors[0][:, h : h + 1]
        partial = partial + nn(paired.astype(bf16), wout_v[h, small:, :])
    red[0] = partial
    reductions = []
    for dh, dp in group:
        code = dh * npr + dp
        copy = pltpu.make_async_remote_copy(
            src_ref=red.at[0],
            dst_ref=red.at[code],
            send_sem=rs_sem.at[code],
            recv_sem=rr_sem.at[code],
            device_id=group_peer(dh, dp),
            device_id_type=MESH,
        )
        copy.start()
        reductions.append(copy)
    for copy in reductions:
        copy.wait()
    update = jnp.zeros((rows, width), f32)
    for h in range(nh):
        for p in range(npr):
            code = lax.rem(me_h - h + nh, nh) * npr + lax.rem(me_p - p + npr, npr)
            update = update + red[code]
    mixed = single.astype(f32) + update
    centre = jnp.mean(mixed, axis=1, keepdims=True)
    away = mixed - centre
    variance = jnp.mean(away * away, axis=1, keepdims=True)
    out = (away * lax.rsqrt(variance + 1e-05) * loaded("gain")[...].reshape(1, width)).astype(bf16)
    so_ref[...] = out
    motion = nt(w_back, out)
    m = [motion[k : k + 1] for k in range(6)]
    inverse = 1.0 / jnp.sqrt(1.0 + m[0] * m[0] + m[1] * m[1] + m[2] * m[2])
    qa, qb, qc, qd = inverse, m[0] * inverse, m[1] * inverse, m[2] * inverse
    spin = [
        qa * qa + qb * qb - qc * qc - qd * qd,
        2.0 * (qb * qc - qa * qd),
        2.0 * (qb * qd + qa * qc),
        2.0 * (qb * qc + qa * qd),
        qa * qa - qb * qb + qc * qc - qd * qd,
        2.0 * (qc * qd - qa * qb),
        2.0 * (qb * qd - qa * qc),
        2.0 * (qc * qd + qa * qb),
        qa * qa - qb * qb - qc * qc + qd * qd,
    ]
    turn = [frames[k : k + 1] for k in range(12)]
    lines = [
        sum(turn[3 * a + b] * spin[3 * b + c] for b in range(3)) for a in range(3) for c in range(3)
    ]
    lines += [
        turn[9 + a] + sum(turn[3 * a + b] * m[3 + b] for b in range(3)) for a in range(3)
    ]
    lines = jnp.concatenate(lines + [jnp.zeros((4, rows), f32)], axis=0)
    fg[me_b] = jnp.concatenate([lines, jnp.zeros((16, LANES - rows), f32)], axis=1)
    finals = []
    for d in range(1, nb):
        copy = pltpu.make_async_remote_copy(
            src_ref=fg.at[me_b],
            dst_ref=fg.at[me_b],
            send_sem=fs_sem.at[d],
            recv_sem=fr_sem.at[d],
            device_id=blk_peer(d),
            device_id_type=MESH,
        )
        copy.start()
        finals.append(copy)
    for copy in finals:
        copy.wait()
    for k in range(nb):
        fo_ref[:, k * rows : (k + 1) * rows] = fg[k, :12, :rows]


def body(
    single, pair, frames, chain, mask, w_query, w_key_value, w_query_points, w_kv_points,
    w_pair_bias, head_weights, chain_bias, w_out, out_gain, w_backbone,
):
    nb, nh, npr = (lax.axis_size(a) for a in ("blk", "head", "pair"))
    rows, width = single.shape
    half = rows // npr
    channels = pair.shape[3]
    heads = w_pair_bias.shape[1]
    size = w_query.shape[1] // heads
    queries = w_query_points.shape[1] // (3 * heads)
    values = w_kv_points.shape[1] // (3 * heads) - queries
    wide = up(heads * max(size, values), LANES)
    dims = (nb, nh, npr, heads, size, queries, values)
    vmem = pl.BlockSpec(memory_space=pltpu.VMEM)
    dma = pltpu.SemaphoreType.DMA
    selected = selectors(heads, size, queries, values)
    given = dict(zip(("sel_q", "sel_kv", "sel_kp", "sel_out"), selected))
    given.update(
        single=single, pair=pair.reshape(rows * nb * half, channels), frames=frames,
        chain_row=chain.reshape(1, rows), mask_row=mask.reshape(1, rows), chain=chain, mask=mask,
        w_q=w_query.T, w_kv=w_key_value.T, w_qp=w_query_points.T, w_kp=w_kv_points.T,
        w_bias=w_pair_bias.T, head_weights=head_weights, chain_bias=chain_bias, w_out=w_out,
        gain=out_gain, w_back=w_backbone.T,
    )
    operands = [given[name] for name in ORDER]
    held = [
        (pltpu.SMEM if name in SCALARS else pltpu.VMEM)(given[name].shape, given[name].dtype)
        for name in ORDER
    ]
    return tuple(
        pl.pallas_call(
            functools.partial(kernel, dims),
            out_shape=(
                jax.ShapeDtypeStruct((rows, width), jnp.bfloat16),
                jax.ShapeDtypeStruct((12, nb * rows), jnp.float32),
            ),
            in_specs=[pl.BlockSpec(memory_space=pl.ANY)] * len(operands),
            out_specs=(vmem, vmem),
            scratch_shapes=held
            + [
                pltpu.VMEM((nb, half, width + LANES), jnp.float32),
                pltpu.VMEM((rows, LANES), jnp.float32),
                pltpu.VMEM((rows * SUB, channels), jnp.float32),
                pltpu.VMEM((npr, rows, LANES + 3 * wide), jnp.float32),
                pltpu.VMEM((nh * npr, rows, width), jnp.float32),
                pltpu.VMEM((nb, 16, LANES), jnp.float32),
                dma((len(operands),)),
                dma((nb,)),
                dma((nb,)),
                dma((npr,)),
                dma((npr,)),
                dma((nh * npr,)),
                dma((nh * npr,)),
                dma((nb,)),
                dma((nb,)),
            ],
            compiler_params=pltpu.CompilerParams(collective_id=0, has_side_effects=True),
        )(*operands)
    )


def solution(mesh):
    placed = (
        P(("groups", "blk"), None),
        P(("groups", "blk"), None, "pair", None),
        P(None, ("groups", "blk")),
        P(("groups", "blk")),
        P(("groups", "blk")),
        P(None, "head"),
        P(None, "head"),
        P(None, "head"),
        P(None, "head"),
        P(None, "head"),
        P("head"),
        P("head"),
        P("head", None, None),
        P(),
        P(),
    )
    return jax.shard_map(
        body,
        mesh=mesh,
        in_specs=placed,
        out_specs=(P(("groups", "blk"), None), P(None, "groups")),
        check_vma=False,
    )
```

```python
import functools
import math

import jax
import jax.numpy as jnp
import numpy as np
from jax import lax
from jax.experimental import pallas as pl
from jax.experimental.pallas import tpu as pltpu
from jax.sharding import PartitionSpec as P

LOGIT_WEIGHT = math.sqrt(1.0 / 3.0)
MASK_PENALTY = 100000.0
MESH = pl.DeviceIdType.MESH
LANES = 128
SUB = 8


def up(value, unit):
    return -(-value // unit) * unit


def nt(a, b):
    return lax.dot_general(a, b, (((1,), (1,)), ((), ())), preferred_element_type=jnp.float32)


def nn(a, b):
    return lax.dot_general(a, b, (((1,), (0,)), ((), ())), preferred_element_type=jnp.float32)


def halves(value):
    high = value.astype(jnp.bfloat16)
    return high, (value - high.astype(jnp.float32)).astype(jnp.bfloat16)


def dot3(product, a, b):
    a_high, a_low = halves(a)
    b_high, b_low = halves(b)
    return product(a_high, b_high) + (product(a_low, b_high) + product(a_high, b_low))


def selectors(heads, size, queries, values):
    wide = up(heads * max(size, values), LANES)
    sel_q = np.zeros((3 * queries * SUB, heads * queries * 3), np.float32)
    key_rows = up(heads * size, 16)
    sel_kv = np.zeros((key_rows + wide, heads * 2 * size), np.float32)
    sel_kp = np.zeros((3 * queries * SUB + 3 * wide, heads * (queries + values) * 3), np.float32)
    small = size + 4 * values
    sel_out = np.zeros((5 * wide, heads * small), np.float32)
    for h in range(heads):
        for b in range(3):
            for p in range(queries):
                row = (b * queries + p) * SUB + h
                sel_q[row, (h * queries + p) * 3 + b] = 1
                sel_kp[row, (h * (queries + values) + p) * 3 + b] = 1
            for p in range(values):
                row = 3 * queries * SUB + b * wide + h * values + p
                sel_kp[row, (h * (queries + values) + queries + p) * 3 + b] = 1
                sel_out[(1 + b) * wide + h * values + p, h * small + size + p * 3 + b] = 1
        for p in range(values):
            sel_out[4 * wide + h * values + p, h * small + size + 3 * values + p] = 1
        for c in range(size):
            sel_kv[h * size + c, h * 2 * size + c] = 1
            sel_kv[key_rows + h * size + c, h * 2 * size + size + c] = 1
            sel_out[h * size + c, h * small + c] = 1
    return [jnp.asarray(s, jnp.bfloat16) for s in (sel_q, sel_kv, sel_kp, sel_out)]


ORDER = (
    "frames", "chain_row", "mask_row", "single", "sel_kv", "w_kv", "sel_kp", "w_kp", "sel_q", "w_qp",
    "w_q", "w_bias", "w_back", "head_weights", "chain_bias", "pair", "w_out", "sel_out", "chain",
    "mask", "gain",
)
SCALARS = ("head_weights", "chain_bias", "chain", "mask")


def kernel(dims, *refs):
    count = len(ORDER)
    far = refs[:count]
    so_ref, fo_ref = refs[count : count + 2]
    near = dict(zip(ORDER, refs[count + 2 : 2 * count + 2]))
    (
        gath, meta_s, sp, ex, part, red, so32, fg,
        load_sem, gs_sem, gr_sem, es_sem, er_sem, rs_sem, rr_sem, fs_sem, fr_sem,
        os_sem, or_sem,
    ) = refs[2 * count + 2 :]
    loads = {
        name: pltpu.make_async_copy(source, near[name], load_sem.at[k])
        for k, (name, source) in enumerate(zip(ORDER, far))
    }

    def loaded(name):
        loads[name].wait()
        return near[name]

    nb, nh, npr, heads, size, queries, values = dims
    rows, width = near["single"].shape
    half = rows // npr
    keys = nb * half
    wide = up(heads * max(size, values), LANES)
    me_b = lax.axis_index("blk")
    me_h = lax.axis_index("head")
    me_p = lax.axis_index("pair")
    f32, bf16 = jnp.float32, jnp.bfloat16

    def block_peer(d, dp):
        return {"blk": lax.rem(me_b + d, nb), "pair": lax.rem(me_p + dp, npr)}

    def group_peer(dh, dp):
        return {"head": lax.rem(me_h + dh, nh), "pair": lax.rem(me_p + dp, npr)}

    block = [(d, dp) for d in range(nb) for dp in range(npr) if d or dp]
    group = [(dh, dp) for dh in range(nh) for dp in range(npr) if dh or dp]
    barrier = pltpu.get_barrier_semaphore()
    for peer in [block_peer(d, dp) for d, dp in block] + [group_peer(dh, dp) for dh, dp in group if dh]:
        pl.semaphore_signal(barrier, inc=1, device_id=peer, device_id_type=MESH)
    for name in ORDER:
        loads[name].start()
    frames = loaded("frames")[...]
    chain_row = loaded("chain_row")[...].astype(f32)
    mask_row = loaded("mask_row")[...].astype(f32)
    single_ref = loaded("single")
    meta = jnp.concatenate(
        [
            frames,
            chain_row,
            mask_row,
            jnp.zeros((LANES - 14, rows), f32),
        ],
        axis=0,
    ).T
    meta_s[...] = meta
    start = pl.multiple_of(me_p * half, half)
    gath[me_b, :, :width] = single_ref[pl.ds(start, half), :].astype(f32)
    gath[me_b, :, width:] = meta_s[pl.ds(start, half), :]
    my_frames = meta_s[pl.ds(start, half), :].T

    single = single_ref[...]
    pl.semaphore_wait(barrier, len(block) + (nh - 1) * npr)
    gathers = []
    upper = (2 * me_b) // nb
    for s in range(nb - 1):
        rising = s + (s - me_b + nb) // nb
        falling = nb - 1 - s - (me_b - (nb - 1 - s) + nb) // nb
        peer = upper * rising + (1 - upper) * falling
        copy = pltpu.make_async_remote_copy(
            src_ref=gath.at[me_b],
            dst_ref=gath.at[me_b],
            send_sem=gs_sem.at[s],
            recv_sem=gr_sem.at[me_b],
            device_id={"blk": peer},
            device_id_type=MESH,
        )
        copy.start()
        landing = pltpu.make_async_remote_copy(
            src_ref=gath.at[peer],
            dst_ref=gath.at[peer],
            send_sem=gs_sem.at[s],
            recv_sem=gr_sem.at[peer],
            device_id={"blk": peer},
            device_id_type=MESH,
        )
        gathers.append((copy, landing))

    w_kv = nn(loaded("sel_kv")[...], loaded("w_kv")[...]).astype(bf16)
    w_kp = nn(loaded("sel_kp")[...], loaded("w_kp")[...]).astype(bf16)
    w_qp = nn(loaded("sel_q")[...], loaded("w_qp")[...]).astype(bf16)
    query = nt(single, loaded("w_q")[...]) * (1.0 / math.sqrt(size))
    q_local = nt(w_qp, single)
    step = queries * SUB

    def moved(local, base, count, turn):
        out = []
        for a in range(3):
            total = turn[9 + a : 10 + a]
            mixed = sum(
                turn[3 * a + b : 3 * a + b + 1] * local[base + b * count : base + (b + 1) * count]
                for b in range(3)
            )
            out.append(mixed + total)
        return out

    q_global = moved(q_local, 0, step, frames)
    eye = (
        lax.broadcasted_iota(jnp.int32, (SUB, heads), 0)
        == lax.broadcasted_iota(jnp.int32, (SUB, heads), 1)
    ).astype(bf16)
    w_bias = nn(eye, loaded("w_bias")[...]).astype(bf16)
    wbb_ref = loaded("w_back")
    eye6 = (
        lax.broadcasted_iota(jnp.int32, (SUB, wbb_ref.shape[0]), 0)
        == lax.broadcasted_iota(jnp.int32, (SUB, wbb_ref.shape[0]), 1)
    ).astype(bf16)
    w_back = nn(eye6, wbb_ref[...]).astype(bf16)
    head_row = lax.broadcasted_iota(jnp.int32, (SUB, keys), 0)
    raw = jnp.zeros((SUB, keys), f32)
    chain_term = jnp.zeros((SUB, keys), f32)
    hw_ref, cb_ref = loaded("head_weights"), loaded("chain_bias")
    for h in range(heads):
        raw = jnp.where(head_row == h, hw_ref[h], raw)
        chain_term = jnp.where(head_row == h, cb_ref[h], chain_term)
    soft = jnp.maximum(raw, 0.0) + jnp.log1p(jnp.exp(-jnp.abs(raw)))
    distance_scale = soft * (math.sqrt(2.0 / (9.0 * queries)) / 2.0)
    own_head = (
        lax.broadcasted_iota(jnp.int32, (SUB, heads * size), 1) // size
        == lax.broadcasted_iota(jnp.int32, (SUB, heads * size), 0)
    ).astype(f32)
    q_wide = (query[:, None, :] * own_head[None]).reshape(rows * SUB, heads * size)
    pair_v = loaded("pair")
    pairs = [pair_v[i * keys : (i + 1) * keys, :] for i in range(rows)]
    biases = [nt(w_bias, pairs[i]) for i in range(rows)]
    wout_v = loaded("w_out")
    small = size + 4 * values
    w_small = nn(
        loaded("sel_out")[...], jnp.concatenate([wout_v[h, :small, :] for h in range(heads)], axis=0)
    ).astype(bf16)

    for copy, landing in gathers:
        landing.wait_recv()
    everyone = gath[...].reshape(keys, width + LANES)
    key_single = everyone[:, :width].astype(bf16)
    key_meta = everyone[:, width:].T
    kv = nt(w_kv, key_single)
    key_rows = up(heads * size, 16)
    kp = nt(w_kp, key_single)
    k_global = moved(kp, 0, step, key_meta)
    v_global = moved(kp, 3 * step, wide, key_meta)
    dots = dot3(nn, q_wide, kv[: heads * size])
    key_chain = jnp.broadcast_to(key_meta[12:13], (SUB, keys))
    key_present = jnp.broadcast_to(key_meta[13:14], (SUB, keys))
    chain_ref, mask_ref = loaded("chain"), loaded("mask")

    weights, tops, totals = [], [], []
    for i in range(rows):
        distance = jnp.zeros((SUB, keys), f32)
        for a in range(3):
            for p in range(queries):
                gap = (
                    q_global[a][p * SUB : (p + 1) * SUB, i : i + 1]
                    - k_global[a][p * SUB : (p + 1) * SUB, :]
                )
                distance = distance + gap * gap
        differ = jnp.where(key_chain != chain_ref[i].astype(f32), chain_term, 0.0)
        logits = LOGIT_WEIGHT * (
            dots[i * SUB : (i + 1) * SUB] + biases[i] - distance_scale * distance + differ
        )
        absent = 1.0 - mask_ref[i].astype(f32) * key_present
        logits = logits - MASK_PENALTY * absent
        top = jnp.max(logits, axis=1, keepdims=True)
        weight = jnp.exp(logits - top)
        weights.append(weight)
        tops.append(jnp.broadcast_to(top, (SUB, LANES)))
        totals.append(jnp.broadcast_to(jnp.sum(weight, axis=1, keepdims=True), (SUB, LANES)))

    lane = lax.broadcasted_iota(jnp.int32, (SUB, LANES), 1)
    row = lax.broadcasted_iota(jnp.int32, (SUB, LANES), 0)
    stat = jnp.concatenate(
        [
            jnp.sum(
                jnp.where(lane == row, tops[i], jnp.where(lane == row + SUB, totals[i], 0.0)),
                axis=0,
                keepdims=True,
            )
            for i in range(rows)
        ],
        axis=0,
    )
    wide_lane = lax.broadcasted_iota(jnp.int32, (SUB, wide), 1)
    wide_row = lax.broadcasted_iota(jnp.int32, (SUB, wide), 0)
    keep_value = (wide_lane // size == wide_row).astype(f32)
    keep_point = (wide_lane // values == wide_row).astype(f32)
    keep = jnp.concatenate([keep_value, keep_point, keep_point, keep_point], axis=1)
    every = jnp.concatenate(weights, axis=0)
    sums = dot3(nt, every, jnp.concatenate([kv[key_rows:]] + v_global, axis=0))
    sums = jnp.sum(sums.reshape(rows, SUB, 4 * wide) * keep[None], axis=1)
    ex[0, :, :LANES] = stat
    ex[0, :, LANES:] = sums[:, wide:]
    exchanges = []
    for d in range(1, npr):
        copy = pltpu.make_async_remote_copy(
            src_ref=ex.at[0],
            dst_ref=ex.at[d],
            send_sem=es_sem.at[d],
            recv_sem=er_sem.at[d],
            device_id=group_peer(0, d),
            device_id_type=MESH,
        )
        copy.start()
        exchanges.append(copy)

    for i in range(rows):
        sp[i * SUB : (i + 1) * SUB, :] = nn(weights[i].astype(bf16), pairs[i])

    for copy in exchanges:
        copy.wait()
    stats = [stat] + [ex[d, :, :LANES] for d in range(1, npr)]
    best = functools.reduce(jnp.maximum, [s[:, :SUB] for s in stats])
    scales = [jnp.exp(s[:, :SUB] - best) for s in stats]
    total = sum(s[:, SUB : 2 * SUB] * scale for s, scale in zip(stats, scales))
    factors = [scale / total for scale in scales]
    full_lane = lax.broadcasted_iota(jnp.int32, (rows, wide), 1)

    def spread(factor, count):
        out = jnp.zeros((rows, wide), f32)
        for h in range(heads):
            out = jnp.where(full_lane // count == h, factor[:, h : h + 1], out)
        return out

    attended = sums[:, :wide] * spread(factors[0], size)
    pointed_global = []
    for a in range(3):
        pointed_global.append(sums[:, (1 + a) * wide : (2 + a) * wide] * spread(factors[0], values))
    for d in range(1, npr):
        scale = spread(factors[d], values)
        for a in range(3):
            base = LANES + a * wide
            pointed_global[a] = pointed_global[a] + ex[d, :, base : base + wide] * scale
    shifted = [pointed_global[a] - meta[:, 9 + a : 10 + a] for a in range(3)]
    pointed = [
        sum(meta[:, 3 * a + b : 3 * a + b + 1] * shifted[a] for a in range(3)) for b in range(3)
    ]
    norms = jnp.sqrt(sum(p * p for p in pointed) + 1.0)
    features = [attended] + [p * (1.0 / npr) for p in pointed + [norms]]
    partial = sum(
        nn(feature.astype(bf16), w_small[k * wide : (k + 1) * wide])
        for k, feature in enumerate(features)
    )
    for h in range(heads):
        paired = sp[pl.ds(h, rows, stride=SUB), :] * factors[0][:, h : h + 1]
        partial = partial + nn(paired.astype(bf16), wout_v[h, small:, :])
    part[...] = partial
    reductions = []
    for dh, dp in group:
        code = dh * npr + dp
        target = pl.multiple_of(lax.rem(me_p + dp, npr) * half, half)
        copy = pltpu.make_async_remote_copy(
            src_ref=part.at[pl.ds(target, half)],
            dst_ref=red.at[code],
            send_sem=rs_sem.at[code],
            recv_sem=rr_sem.at[code],
            device_id=group_peer(dh, dp),
            device_id_type=MESH,
        )
        copy.start()
        reductions.append(copy)
    red[0] = part[pl.ds(start, half), :]
    for copy, landing in gathers:
        copy.wait_send()
    for copy in reductions:
        copy.wait()
    update = jnp.zeros((half, width), f32)
    for h in range(nh):
        for p in range(npr):
            code = lax.rem(me_h - h + nh, nh) * npr + lax.rem(me_p - p + npr, npr)
            update = update + red[code]
    mixed = gath[me_b, :, :width] + update
    centre = jnp.mean(mixed, axis=1, keepdims=True)
    away = mixed - centre
    variance = jnp.mean(away * away, axis=1, keepdims=True)
    out = (away * lax.rsqrt(variance + 1e-05) * loaded("gain")[...].reshape(1, width)).astype(bf16)
    motion = nt(w_back, out)
    m = [motion[k : k + 1] for k in range(6)]
    inverse = 1.0 / jnp.sqrt(1.0 + m[0] * m[0] + m[1] * m[1] + m[2] * m[2])
    qa, qb, qc, qd = inverse, m[0] * inverse, m[1] * inverse, m[2] * inverse
    spin = [
        qa * qa + qb * qb - qc * qc - qd * qd,
        2.0 * (qb * qc - qa * qd),
        2.0 * (qb * qd + qa * qc),
        2.0 * (qb * qc + qa * qd),
        qa * qa - qb * qb + qc * qc - qd * qd,
        2.0 * (qc * qd - qa * qb),
        2.0 * (qb * qd - qa * qc),
        2.0 * (qc * qd + qa * qb),
        qa * qa - qb * qb - qc * qc + qd * qd,
    ]
    turn = [my_frames[k : k + 1] for k in range(12)]
    lines = [
        sum(turn[3 * a + b] * spin[3 * b + c] for b in range(3)) for a in range(3) for c in range(3)
    ]
    lines += [
        turn[9 + a] + sum(turn[3 * a + b] * m[3 + b] for b in range(3)) for a in range(3)
    ]
    lines = jnp.concatenate(lines + [jnp.zeros((4, half), f32)], axis=0)
    fg[me_b, me_p] = jnp.concatenate([lines, jnp.zeros((16, LANES - half), f32)], axis=1)
    finals = []
    for d, dp in block:
        code = d * npr + dp
        copy = pltpu.make_async_remote_copy(
            src_ref=fg.at[me_b, me_p],
            dst_ref=fg.at[me_b, me_p],
            send_sem=fs_sem.at[code],
            recv_sem=fr_sem.at[code],
            device_id=block_peer(d, dp),
            device_id_type=MESH,
        )
        copy.start()
        finals.append(copy)
    so32[me_p] = out.astype(f32)
    for d in range(1, npr):
        copy = pltpu.make_async_remote_copy(
            src_ref=so32.at[me_p],
            dst_ref=so32.at[me_p],
            send_sem=os_sem.at[d],
            recv_sem=or_sem.at[d],
            device_id=group_peer(0, d),
            device_id_type=MESH,
        )
        copy.start()
        finals.append(copy)
    for copy in finals[len(block) :]:
        copy.wait()
    for p in range(npr):
        so_ref[p * half : (p + 1) * half, :] = so32[p].astype(bf16)
    for copy in finals[: len(block)]:
        copy.wait()
    for k in range(nb):
        for p in range(npr):
            spot = (k * npr + p) * half
            fo_ref[:, spot : spot + half] = fg[k, p, :12, :half]


def body(
    single, pair, frames, chain, mask, w_query, w_key_value, w_query_points, w_kv_points,
    w_pair_bias, head_weights, chain_bias, w_out, out_gain, w_backbone,
):
    nb, nh, npr = (lax.axis_size(a) for a in ("blk", "head", "pair"))
    rows, width = single.shape
    half = rows // npr
    channels = pair.shape[3]
    heads = w_pair_bias.shape[1]
    size = w_query.shape[1] // heads
    queries = w_query_points.shape[1] // (3 * heads)
    values = w_kv_points.shape[1] // (3 * heads) - queries
    wide = up(heads * max(size, values), LANES)
    dims = (nb, nh, npr, heads, size, queries, values)
    vmem = pl.BlockSpec(memory_space=pltpu.VMEM)
    dma = pltpu.SemaphoreType.DMA
    selected = selectors(heads, size, queries, values)
    given = dict(zip(("sel_q", "sel_kv", "sel_kp", "sel_out"), selected))
    given.update(
        single=single, pair=pair.reshape(rows * nb * half, channels), frames=frames,
        chain_row=chain.reshape(1, rows), mask_row=mask.reshape(1, rows), chain=chain, mask=mask,
        w_q=w_query.T, w_kv=w_key_value.T, w_qp=w_query_points.T, w_kp=w_kv_points.T,
        w_bias=w_pair_bias.T, head_weights=head_weights, chain_bias=chain_bias, w_out=w_out,
        gain=out_gain, w_back=w_backbone.T,
    )
    operands = [given[name] for name in ORDER]
    held = [
        (pltpu.SMEM if name in SCALARS else pltpu.VMEM)(given[name].shape, given[name].dtype)
        for name in ORDER
    ]
    return tuple(
        pl.pallas_call(
            functools.partial(kernel, dims),
            out_shape=(
                jax.ShapeDtypeStruct((rows, width), jnp.bfloat16),
                jax.ShapeDtypeStruct((12, nb * rows), jnp.float32),
            ),
            in_specs=[pl.BlockSpec(memory_space=pl.ANY)] * len(operands),
            out_specs=(vmem, vmem),
            scratch_shapes=held
            + [
                pltpu.VMEM((nb, half, width + LANES), jnp.float32),
                pltpu.VMEM((rows, LANES), jnp.float32),
                pltpu.VMEM((rows * SUB, channels), jnp.float32),
                pltpu.VMEM((npr, rows, LANES + 3 * wide), jnp.float32),
                pltpu.VMEM((rows, width), jnp.float32),
                pltpu.VMEM((nh * npr, half, width), jnp.float32),
                pltpu.VMEM((npr, half, width), jnp.float32),
                pltpu.VMEM((nb, npr, 16, LANES), jnp.float32),
                dma((len(operands),)),
                dma((nb,)),
                dma((nb,)),
                dma((npr,)),
                dma((npr,)),
                dma((nh * npr,)),
                dma((nh * npr,)),
                dma((nb * npr,)),
                dma((nb * npr,)),
                dma((npr,)),
                dma((npr,)),
            ],
            compiler_params=pltpu.CompilerParams(collective_id=0, has_side_effects=True),
        )(*operands)
    )


def solution(mesh):
    placed = (
        P(("groups", "blk"), None),
        P(("groups", "blk"), None, "pair", None),
        P(None, ("groups", "blk")),
        P(("groups", "blk")),
        P(("groups", "blk")),
        P(None, "head"),
        P(None, "head"),
        P(None, "head"),
        P(None, "head"),
        P(None, "head"),
        P("head"),
        P("head"),
        P("head", None, None),
        P(),
        P(),
    )
    return jax.shard_map(
        body,
        mesh=mesh,
        in_specs=placed,
        out_specs=(P(("groups", "blk"), None), P(None, "groups")),
        check_vma=False,
    )
```

```python
import functools
import math

import jax
import jax.numpy as jnp
import numpy as np
from jax import lax
from jax.experimental import pallas as pl
from jax.experimental.pallas import tpu as pltpu
from jax.sharding import PartitionSpec as P

LOGIT_WEIGHT = math.sqrt(1.0 / 3.0)
MASK_PENALTY = 100000.0
MESH = pl.DeviceIdType.MESH
LANES = 128
SUB = 8


def up(value, unit):
    return -(-value // unit) * unit


def nt(a, b):
    return lax.dot_general(a, b, (((1,), (1,)), ((), ())), preferred_element_type=jnp.float32)


def nn(a, b):
    return lax.dot_general(a, b, (((1,), (0,)), ((), ())), preferred_element_type=jnp.float32)


def halves(value):
    high = value.astype(jnp.bfloat16)
    return high, (value - high.astype(jnp.float32)).astype(jnp.bfloat16)


def dot3(product, a, b):
    a_high, a_low = halves(a)
    b_high, b_low = halves(b)
    return product(a_high, b_high) + (product(a_low, b_high) + product(a_high, b_low))


def selectors(heads, size, queries, values):
    wide = up(heads * max(size, values), LANES)
    sel_q = np.zeros((3 * queries * SUB, heads * queries * 3), np.float32)
    key_rows = up(heads * size, 16)
    sel_kv = np.zeros((key_rows + wide, heads * 2 * size), np.float32)
    sel_kp = np.zeros((3 * queries * SUB + 3 * wide, heads * (queries + values) * 3), np.float32)
    small = size + 4 * values
    sel_out = np.zeros((5 * wide, heads * small), np.float32)
    for h in range(heads):
        for b in range(3):
            for p in range(queries):
                row = (b * queries + p) * SUB + h
                sel_q[row, (h * queries + p) * 3 + b] = 1
                sel_kp[row, (h * (queries + values) + p) * 3 + b] = 1
            for p in range(values):
                row = 3 * queries * SUB + b * wide + h * values + p
                sel_kp[row, (h * (queries + values) + queries + p) * 3 + b] = 1
                sel_out[(1 + b) * wide + h * values + p, h * small + size + p * 3 + b] = 1
        for p in range(values):
            sel_out[4 * wide + h * values + p, h * small + size + 3 * values + p] = 1
        for c in range(size):
            sel_kv[h * size + c, h * 2 * size + c] = 1
            sel_kv[key_rows + h * size + c, h * 2 * size + size + c] = 1
            sel_out[h * size + c, h * small + c] = 1
    return [jnp.asarray(s, jnp.bfloat16) for s in (sel_q, sel_kv, sel_kp, sel_out)]


ORDER = (
    "frames", "chain_row", "mask_row", "single", "sel_kv", "w_kv", "sel_kp", "w_kp", "sel_q", "w_qp",
    "w_q", "w_bias", "w_back", "head_weights", "chain_bias", "pair", "w_out", "sel_out", "chain",
    "mask", "gain",
)
SCALARS = ("head_weights", "chain_bias", "chain", "mask")


def kernel(dims, *refs):
    count = len(ORDER)
    far = refs[:count]
    so_ref, fo_ref = refs[count : count + 2]
    near = dict(zip(ORDER, refs[count + 2 : 2 * count + 2]))
    (
        gath, meta_s, qb, sp, ex, part, red, so32, fg,
        load_sem, gs_sem, gr_sem, es_sem, er_sem, rs_sem, rr_sem, fs_sem, fr_sem,
        os_sem, or_sem,
    ) = refs[2 * count + 2 :]
    loads = {
        name: pltpu.make_async_copy(source, near[name], load_sem.at[k])
        for k, (name, source) in enumerate(zip(ORDER, far))
    }

    def loaded(name):
        loads[name].wait()
        return near[name]

    nb, nh, npr, heads, size, queries, values = dims
    rows, width = near["single"].shape
    half = rows // npr
    keys = nb * half
    wide = up(heads * max(size, values), LANES)
    me_b = lax.axis_index("blk")
    me_h = lax.axis_index("head")
    me_p = lax.axis_index("pair")
    f32, bf16 = jnp.float32, jnp.bfloat16

    def block_peer(d, dp):
        return {"blk": lax.rem(me_b + d, nb), "pair": lax.rem(me_p + dp, npr)}

    def group_peer(dh, dp):
        return {"head": lax.rem(me_h + dh, nh), "pair": lax.rem(me_p + dp, npr)}

    block = [(d, dp) for d in range(nb) for dp in range(npr) if d or dp]
    group = [(dh, dp) for dh in range(nh) for dp in range(npr) if dh or dp]
    barrier = pltpu.get_barrier_semaphore()
    for peer in [block_peer(d, dp) for d, dp in block] + [group_peer(dh, dp) for dh, dp in group if dh]:
        pl.semaphore_signal(barrier, inc=1, device_id=peer, device_id_type=MESH)
    for name in ORDER:
        loads[name].start()
    frames = loaded("frames")[...]
    chain_row = loaded("chain_row")[...].astype(f32)
    mask_row = loaded("mask_row")[...].astype(f32)
    single_ref = loaded("single")
    meta = jnp.concatenate(
        [
            frames,
            chain_row,
            mask_row,
            jnp.zeros((LANES - 14, rows), f32),
        ],
        axis=0,
    ).T
    meta_s[...] = meta
    start = pl.multiple_of(me_p * half, half)
    gath[me_b, :, :width] = single_ref[pl.ds(start, half), :].astype(f32)
    gath[me_b, :, width:] = meta_s[pl.ds(start, half), :]
    my_frames = meta_s[pl.ds(start, half), :].T

    single = single_ref[...]
    pl.semaphore_wait(barrier, len(block) + (nh - 1) * npr)
    gathers = []
    upper = (2 * me_b) // nb
    for s in range(nb - 1):
        rising = s + (s - me_b + nb) // nb
        falling = nb - 1 - s - (me_b - (nb - 1 - s) + nb) // nb
        peer = upper * rising + (1 - upper) * falling
        copy = pltpu.make_async_remote_copy(
            src_ref=gath.at[me_b],
            dst_ref=gath.at[me_b],
            send_sem=gs_sem.at[s],
            recv_sem=gr_sem.at[me_b],
            device_id={"blk": peer},
            device_id_type=MESH,
        )
        copy.start()
        landing = pltpu.make_async_remote_copy(
            src_ref=gath.at[peer],
            dst_ref=gath.at[peer],
            send_sem=gs_sem.at[s],
            recv_sem=gr_sem.at[peer],
            device_id={"blk": peer},
            device_id_type=MESH,
        )
        gathers.append((copy, landing))

    w_kv = nn(loaded("sel_kv")[...], loaded("w_kv")[...]).astype(bf16)
    w_kp = nn(loaded("sel_kp")[...], loaded("w_kp")[...]).astype(bf16)
    w_qp = nn(loaded("sel_q")[...], loaded("w_qp")[...]).astype(bf16)
    query = nt(single, loaded("w_q")[...]) * (1.0 / math.sqrt(size))
    q_local = nt(w_qp, single)
    step = queries * SUB

    def moved(local, base, count, turn):
        out = []
        for a in range(3):
            total = turn[9 + a : 10 + a]
            mixed = sum(
                turn[3 * a + b : 3 * a + b + 1] * local[base + b * count : base + (b + 1) * count]
                for b in range(3)
            )
            out.append(mixed + total)
        return out

    q_global = moved(q_local, 0, step, frames)
    for a in range(3):
        for p in range(queries):
            for i in range(rows):
                spot = ((a * queries + p) * rows + i) * SUB
                qb[spot : spot + SUB, :] = jnp.broadcast_to(
                    q_global[a][p * SUB : (p + 1) * SUB, i : i + 1], (SUB, LANES)
                )

    def along_keys(value):
        if keys <= LANES:
            return value[:, :keys]
        return jnp.concatenate([value] * (keys // LANES), axis=1)

    eye = (
        lax.broadcasted_iota(jnp.int32, (SUB, heads), 0)
        == lax.broadcasted_iota(jnp.int32, (SUB, heads), 1)
    ).astype(bf16)
    w_bias = nn(eye, loaded("w_bias")[...]).astype(bf16)
    wbb_ref = loaded("w_back")
    eye6 = (
        lax.broadcasted_iota(jnp.int32, (SUB, wbb_ref.shape[0]), 0)
        == lax.broadcasted_iota(jnp.int32, (SUB, wbb_ref.shape[0]), 1)
    ).astype(bf16)
    w_back = nn(eye6, wbb_ref[...]).astype(bf16)
    head_row = lax.broadcasted_iota(jnp.int32, (SUB, keys), 0)
    raw = jnp.zeros((SUB, keys), f32)
    chain_term = jnp.zeros((SUB, keys), f32)
    hw_ref, cb_ref = loaded("head_weights"), loaded("chain_bias")
    for h in range(heads):
        raw = jnp.where(head_row == h, hw_ref[h], raw)
        chain_term = jnp.where(head_row == h, cb_ref[h], chain_term)
    soft = jnp.maximum(raw, 0.0) + jnp.log1p(jnp.exp(-jnp.abs(raw)))
    distance_scale = soft * (math.sqrt(2.0 / (9.0 * queries)) / 2.0)
    own_head = (
        lax.broadcasted_iota(jnp.int32, (SUB, heads * size), 1) // size
        == lax.broadcasted_iota(jnp.int32, (SUB, heads * size), 0)
    ).astype(f32)
    q_wide = (query[:, None, :] * own_head[None]).reshape(rows * SUB, heads * size)
    pair_v = loaded("pair")
    pairs = [pair_v[i * keys : (i + 1) * keys, :] for i in range(rows)]
    biases = [nt(w_bias, pairs[i]) for i in range(rows)]
    wout_v = loaded("w_out")
    small = size + 4 * values
    w_small = nn(
        loaded("sel_out")[...], jnp.concatenate([wout_v[h, :small, :] for h in range(heads)], axis=0)
    ).astype(bf16)

    for copy, landing in gathers:
        landing.wait_recv()
    everyone = gath[...].reshape(keys, width + LANES)
    key_single = everyone[:, :width].astype(bf16)
    key_meta = everyone[:, width:].T
    kv = nt(w_kv, key_single)
    key_rows = up(heads * size, 16)
    kp = nt(w_kp, key_single)
    k_global = moved(kp, 0, step, key_meta)
    v_global = moved(kp, 3 * step, wide, key_meta)
    dots = dot3(nn, q_wide, kv[: heads * size])
    key_chain = jnp.broadcast_to(key_meta[12:13], (SUB, keys))
    key_present = jnp.broadcast_to(key_meta[13:14], (SUB, keys))
    chain_ref, mask_ref = loaded("chain"), loaded("mask")

    weights, tops, totals = [], [], []
    for i in range(rows):
        distance = jnp.zeros((SUB, keys), f32)
        for a in range(3):
            for p in range(queries):
                spot = ((a * queries + p) * rows + i) * SUB
                gap = along_keys(qb[spot : spot + SUB, :]) - k_global[a][p * SUB : (p + 1) * SUB, :]
                distance = distance + gap * gap
        differ = jnp.where(key_chain != chain_ref[i].astype(f32), chain_term, 0.0)
        logits = LOGIT_WEIGHT * (
            dots[i * SUB : (i + 1) * SUB] + biases[i] - distance_scale * distance + differ
        )
        absent = 1.0 - mask_ref[i].astype(f32) * key_present
        logits = logits - MASK_PENALTY * absent
        top = jnp.max(logits, axis=1, keepdims=True)
        weight = jnp.exp(logits - top)
        weights.append(weight)
        tops.append(jnp.broadcast_to(top, (SUB, LANES)))
        totals.append(jnp.broadcast_to(jnp.sum(weight, axis=1, keepdims=True), (SUB, LANES)))

    lane = lax.broadcasted_iota(jnp.int32, (SUB, LANES), 1)
    row = lax.broadcasted_iota(jnp.int32, (SUB, LANES), 0)
    stat = jnp.concatenate(
        [
            jnp.sum(
                jnp.where(lane == row, tops[i], jnp.where(lane == row + SUB, totals[i], 0.0)),
                axis=0,
                keepdims=True,
            )
            for i in range(rows)
        ],
        axis=0,
    )
    wide_lane = lax.broadcasted_iota(jnp.int32, (SUB, wide), 1)
    wide_row = lax.broadcasted_iota(jnp.int32, (SUB, wide), 0)
    keep_value = (wide_lane // size == wide_row).astype(f32)
    keep_point = (wide_lane // values == wide_row).astype(f32)
    keep = jnp.concatenate([keep_value, keep_point, keep_point, keep_point], axis=1)
    every = jnp.concatenate(weights, axis=0)
    sums = dot3(nt, every, jnp.concatenate([kv[key_rows:]] + v_global, axis=0))
    sums = jnp.sum(sums.reshape(rows, SUB, 4 * wide) * keep[None], axis=1)
    ex[0, :, :LANES] = stat
    ex[0, :, LANES:] = sums[:, wide:]
    exchanges = []
    for d in range(1, npr):
        copy = pltpu.make_async_remote_copy(
            src_ref=ex.at[0],
            dst_ref=ex.at[d],
            send_sem=es_sem.at[d],
            recv_sem=er_sem.at[d],
            device_id=group_peer(0, d),
            device_id_type=MESH,
        )
        copy.start()
        exchanges.append(copy)

    for i in range(rows):
        sp[i * SUB : (i + 1) * SUB, :] = nn(weights[i].astype(bf16), pairs[i])

    for copy in exchanges:
        copy.wait()
    stats = [stat] + [ex[d, :, :LANES] for d in range(1, npr)]
    best = functools.reduce(jnp.maximum, [s[:, :SUB] for s in stats])
    scales = [jnp.exp(s[:, :SUB] - best) for s in stats]
    total = sum(s[:, SUB : 2 * SUB] * scale for s, scale in zip(stats, scales))
    factors = [scale / total for scale in scales]
    full_lane = lax.broadcasted_iota(jnp.int32, (rows, wide), 1)

    def spread(factor, count):
        out = jnp.zeros((rows, wide), f32)
        for h in range(heads):
            out = jnp.where(full_lane // count == h, factor[:, h : h + 1], out)
        return out

    attended = sums[:, :wide] * spread(factors[0], size)
    pointed_global = []
    for a in range(3):
        pointed_global.append(sums[:, (1 + a) * wide : (2 + a) * wide] * spread(factors[0], values))
    for d in range(1, npr):
        scale = spread(factors[d], values)
        for a in range(3):
            base = LANES + a * wide
            pointed_global[a] = pointed_global[a] + ex[d, :, base : base + wide] * scale
    shifted = [pointed_global[a] - meta[:, 9 + a : 10 + a] for a in range(3)]
    pointed = [
        sum(meta[:, 3 * a + b : 3 * a + b + 1] * shifted[a] for a in range(3)) for b in range(3)
    ]
    norms = jnp.sqrt(sum(p * p for p in pointed) + 1.0)
    features = [attended] + [p * (1.0 / npr) for p in pointed + [norms]]
    partial = sum(
        nn(feature.astype(bf16), w_small[k * wide : (k + 1) * wide])
        for k, feature in enumerate(features)
    )
    for h in range(heads):
        paired = sp[pl.ds(h, rows, stride=SUB), :] * factors[0][:, h : h + 1]
        partial = partial + nn(paired.astype(bf16), wout_v[h, small:, :])
    part[...] = partial
    reductions = []
    for dh, dp in group:
        code = dh * npr + dp
        target = pl.multiple_of(lax.rem(me_p + dp, npr) * half, half)
        copy = pltpu.make_async_remote_copy(
            src_ref=part.at[pl.ds(target, half)],
            dst_ref=red.at[code],
            send_sem=rs_sem.at[code],
            recv_sem=rr_sem.at[code],
            device_id=group_peer(dh, dp),
            device_id_type=MESH,
        )
        copy.start()
        reductions.append(copy)
    red[0] = part[pl.ds(start, half), :]
    for copy, landing in gathers:
        copy.wait_send()
    for copy in reductions:
        copy.wait()
    update = jnp.zeros((half, width), f32)
    for h in range(nh):
        for p in range(npr):
            code = lax.rem(me_h - h + nh, nh) * npr + lax.rem(me_p - p + npr, npr)
            update = update + red[code]
    mixed = gath[me_b, :, :width] + update
    centre = jnp.mean(mixed, axis=1, keepdims=True)
    away = mixed - centre
    variance = jnp.mean(away * away, axis=1, keepdims=True)
    out = (away * lax.rsqrt(variance + 1e-05) * loaded("gain")[...].reshape(1, width)).astype(bf16)
    motion = nt(w_back, out)
    m = [motion[k : k + 1] for k in range(6)]
    inverse = 1.0 / jnp.sqrt(1.0 + m[0] * m[0] + m[1] * m[1] + m[2] * m[2])
    qa, qb, qc, qd = inverse, m[0] * inverse, m[1] * inverse, m[2] * inverse
    spin = [
        qa * qa + qb * qb - qc * qc - qd * qd,
        2.0 * (qb * qc - qa * qd),
        2.0 * (qb * qd + qa * qc),
        2.0 * (qb * qc + qa * qd),
        qa * qa - qb * qb + qc * qc - qd * qd,
        2.0 * (qc * qd - qa * qb),
        2.0 * (qb * qd - qa * qc),
        2.0 * (qc * qd + qa * qb),
        qa * qa - qb * qb - qc * qc + qd * qd,
    ]
    turn = [my_frames[k : k + 1] for k in range(12)]
    lines = [
        sum(turn[3 * a + b] * spin[3 * b + c] for b in range(3)) for a in range(3) for c in range(3)
    ]
    lines += [
        turn[9 + a] + sum(turn[3 * a + b] * m[3 + b] for b in range(3)) for a in range(3)
    ]
    lines = jnp.concatenate(lines + [jnp.zeros((4, half), f32)], axis=0)
    fg[me_b, me_p] = jnp.concatenate([lines, jnp.zeros((16, LANES - half), f32)], axis=1)
    finals = []
    for d, dp in block:
        code = d * npr + dp
        copy = pltpu.make_async_remote_copy(
            src_ref=fg.at[me_b, me_p],
            dst_ref=fg.at[me_b, me_p],
            send_sem=fs_sem.at[code],
            recv_sem=fr_sem.at[code],
            device_id=block_peer(d, dp),
            device_id_type=MESH,
        )
        copy.start()
        finals.append(copy)
    so32[me_p] = out.astype(f32)
    for d in range(1, npr):
        copy = pltpu.make_async_remote_copy(
            src_ref=so32.at[me_p],
            dst_ref=so32.at[me_p],
            send_sem=os_sem.at[d],
            recv_sem=or_sem.at[d],
            device_id=group_peer(0, d),
            device_id_type=MESH,
        )
        copy.start()
        finals.append(copy)
    for copy in finals[len(block) :]:
        copy.wait()
    for p in range(npr):
        so_ref[p * half : (p + 1) * half, :] = so32[p].astype(bf16)
    for copy in finals[: len(block)]:
        copy.wait()
    for k in range(nb):
        for p in range(npr):
            spot = (k * npr + p) * half
            fo_ref[:, spot : spot + half] = fg[k, p, :12, :half]


def body(
    single, pair, frames, chain, mask, w_query, w_key_value, w_query_points, w_kv_points,
    w_pair_bias, head_weights, chain_bias, w_out, out_gain, w_backbone,
):
    nb, nh, npr = (lax.axis_size(a) for a in ("blk", "head", "pair"))
    rows, width = single.shape
    half = rows // npr
    channels = pair.shape[3]
    heads = w_pair_bias.shape[1]
    size = w_query.shape[1] // heads
    queries = w_query_points.shape[1] // (3 * heads)
    values = w_kv_points.shape[1] // (3 * heads) - queries
    wide = up(heads * max(size, values), LANES)
    dims = (nb, nh, npr, heads, size, queries, values)
    vmem = pl.BlockSpec(memory_space=pltpu.VMEM)
    dma = pltpu.SemaphoreType.DMA
    selected = selectors(heads, size, queries, values)
    given = dict(zip(("sel_q", "sel_kv", "sel_kp", "sel_out"), selected))
    given.update(
        single=single, pair=pair.reshape(rows * nb * half, channels), frames=frames,
        chain_row=chain.reshape(1, rows), mask_row=mask.reshape(1, rows), chain=chain, mask=mask,
        w_q=w_query.T, w_kv=w_key_value.T, w_qp=w_query_points.T, w_kp=w_kv_points.T,
        w_bias=w_pair_bias.T, head_weights=head_weights, chain_bias=chain_bias, w_out=w_out,
        gain=out_gain, w_back=w_backbone.T,
    )
    operands = [given[name] for name in ORDER]
    held = [
        (pltpu.SMEM if name in SCALARS else pltpu.VMEM)(given[name].shape, given[name].dtype)
        for name in ORDER
    ]
    return tuple(
        pl.pallas_call(
            functools.partial(kernel, dims),
            out_shape=(
                jax.ShapeDtypeStruct((rows, width), jnp.bfloat16),
                jax.ShapeDtypeStruct((12, nb * rows), jnp.float32),
            ),
            in_specs=[pl.BlockSpec(memory_space=pl.ANY)] * len(operands),
            out_specs=(vmem, vmem),
            scratch_shapes=held
            + [
                pltpu.VMEM((nb, half, width + LANES), jnp.float32),
                pltpu.VMEM((rows, LANES), jnp.float32),
                pltpu.VMEM((3 * queries * rows * SUB, LANES), jnp.float32),
                pltpu.VMEM((rows * SUB, channels), jnp.float32),
                pltpu.VMEM((npr, rows, LANES + 3 * wide), jnp.float32),
                pltpu.VMEM((rows, width), jnp.float32),
                pltpu.VMEM((nh * npr, half, width), jnp.float32),
                pltpu.VMEM((npr, half, width), jnp.float32),
                pltpu.VMEM((nb, npr, 16, LANES), jnp.float32),
                dma((len(operands),)),
                dma((nb,)),
                dma((nb,)),
                dma((npr,)),
                dma((npr,)),
                dma((nh * npr,)),
                dma((nh * npr,)),
                dma((nb * npr,)),
                dma((nb * npr,)),
                dma((npr,)),
                dma((npr,)),
            ],
            compiler_params=pltpu.CompilerParams(collective_id=0, has_side_effects=True),
        )(*operands)
    )


def solution(mesh):
    placed = (
        P(("groups", "blk"), None),
        P(("groups", "blk"), None, "pair", None),
        P(None, ("groups", "blk")),
        P(("groups", "blk")),
        P(("groups", "blk")),
        P(None, "head"),
        P(None, "head"),
        P(None, "head"),
        P(None, "head"),
        P(None, "head"),
        P("head"),
        P("head"),
        P("head", None, None),
        P(),
        P(),
    )
    return jax.shard_map(
        body,
        mesh=mesh,
        in_specs=placed,
        out_specs=(P(("groups", "blk"), None), P(None, "groups")),
        check_vma=False,
    )
```

```python
import functools
import math

import jax
import jax.numpy as jnp
import numpy as np
from jax import lax
from jax.experimental import pallas as pl
from jax.experimental.pallas import tpu as pltpu
from jax.sharding import PartitionSpec as P

LOGIT_WEIGHT = math.sqrt(1.0 / 3.0)
MASK_PENALTY = 100000.0
MESH = pl.DeviceIdType.MESH
LANES = 128
SUB = 8


def up(value, unit):
    return -(-value // unit) * unit


def nt(a, b):
    return lax.dot_general(a, b, (((1,), (1,)), ((), ())), preferred_element_type=jnp.float32)


def nn(a, b):
    return lax.dot_general(a, b, (((1,), (0,)), ((), ())), preferred_element_type=jnp.float32)


def halves(value):
    high = value.astype(jnp.bfloat16)
    return high, (value - high.astype(jnp.float32)).astype(jnp.bfloat16)


def dot3(product, a, b):
    a_high, a_low = halves(a)
    b_high, b_low = halves(b)
    return product(a_high, b_high) + (product(a_low, b_high) + product(a_high, b_low))


def selectors(heads, size, queries, values):
    wide = up(heads * max(size, values), LANES)
    sel_q = np.zeros((3 * queries * SUB, heads * queries * 3), np.float32)
    key_rows = up(heads * size, 16)
    sel_kv = np.zeros((key_rows + wide, heads * 2 * size), np.float32)
    sel_kp = np.zeros((3 * queries * SUB + 3 * wide, heads * (queries + values) * 3), np.float32)
    small = size + 4 * values
    sel_out = np.zeros((5 * wide, heads * small), np.float32)
    for h in range(heads):
        for b in range(3):
            for p in range(queries):
                row = (b * queries + p) * SUB + h
                sel_q[row, (h * queries + p) * 3 + b] = 1
                sel_kp[row, (h * (queries + values) + p) * 3 + b] = 1
            for p in range(values):
                row = 3 * queries * SUB + b * wide + h * values + p
                sel_kp[row, (h * (queries + values) + queries + p) * 3 + b] = 1
                sel_out[(1 + b) * wide + h * values + p, h * small + size + p * 3 + b] = 1
        for p in range(values):
            sel_out[4 * wide + h * values + p, h * small + size + 3 * values + p] = 1
        for c in range(size):
            sel_kv[h * size + c, h * 2 * size + c] = 1
            sel_kv[key_rows + h * size + c, h * 2 * size + size + c] = 1
            sel_out[h * size + c, h * small + c] = 1
    return [jnp.asarray(s, jnp.bfloat16) for s in (sel_q, sel_kv, sel_kp, sel_out)]


ORDER = (
    "frames", "chain_row", "mask_row", "single", "sel_kv", "w_kv", "sel_kp", "w_kp", "sel_q", "w_qp",
    "w_q", "w_bias", "w_back", "head_weights", "chain_bias", "pair", "w_out", "sel_out", "chain",
    "mask", "gain",
)
SCALARS = ("head_weights", "chain_bias", "chain", "mask")


def kernel(dims, *refs):
    count = len(ORDER)
    far = refs[:count]
    so_ref, fo_ref = refs[count : count + 2]
    near = dict(zip(ORDER, refs[count + 2 : 2 * count + 2]))
    (
        gath, meta_s, qb, sp, ex, part, red, so32, fg,
        load_sem, gs_sem, gr_sem, es_sem, er_sem, rs_sem, rr_sem, fs_sem, fr_sem,
        os_sem, or_sem,
    ) = refs[2 * count + 2 :]
    loads = {
        name: pltpu.make_async_copy(source, near[name], load_sem.at[k])
        for k, (name, source) in enumerate(zip(ORDER, far))
    }

    def loaded(name):
        loads[name].wait()
        return near[name]

    nb, nh, npr, heads, size, queries, values = dims
    rows, width = near["single"].shape
    half = rows // npr
    keys = nb * half
    wide = up(heads * max(size, values), LANES)
    me_b = lax.axis_index("blk")
    me_h = lax.axis_index("head")
    me_p = lax.axis_index("pair")
    f32, bf16 = jnp.float32, jnp.bfloat16

    def block_peer(d, dp):
        return {"blk": lax.rem(me_b + d, nb), "pair": lax.rem(me_p + dp, npr)}

    def group_peer(dh, dp):
        return {"head": lax.rem(me_h + dh, nh), "pair": lax.rem(me_p + dp, npr)}

    block = [(d, dp) for d in range(nb) for dp in range(npr) if d or dp]
    group = [(dh, dp) for dh in range(nh) for dp in range(npr) if dh or dp]
    barrier = pltpu.get_barrier_semaphore()
    for peer in [block_peer(d, dp) for d, dp in block] + [group_peer(dh, dp) for dh, dp in group if dh]:
        pl.semaphore_signal(barrier, inc=1, device_id=peer, device_id_type=MESH)
    for name in ORDER:
        loads[name].start()
    frames = loaded("frames")[...]
    chain_row = loaded("chain_row")[...].astype(f32)
    mask_row = loaded("mask_row")[...].astype(f32)
    single_ref = loaded("single")
    meta = jnp.concatenate(
        [
            frames,
            chain_row,
            mask_row,
            jnp.zeros((LANES - 14, rows), f32),
        ],
        axis=0,
    ).T
    meta_s[...] = meta
    start = pl.multiple_of(me_p * half, half)
    gath[me_b, :, :width] = single_ref[pl.ds(start, half), :].astype(f32)
    gath[me_b, :, width:] = meta_s[pl.ds(start, half), :]
    my_frames = meta_s[pl.ds(start, half), :].T

    single = single_ref[...]
    pl.semaphore_wait(barrier, len(block) + (nh - 1) * npr)
    gathers = []
    upper = (2 * me_b) // nb
    for s in range(nb - 1):
        rising = s + (s - me_b + nb) // nb
        falling = nb - 1 - s - (me_b - (nb - 1 - s) + nb) // nb
        peer = upper * rising + (1 - upper) * falling
        copy = pltpu.make_async_remote_copy(
            src_ref=gath.at[me_b],
            dst_ref=gath.at[me_b],
            send_sem=gs_sem.at[s],
            recv_sem=gr_sem.at[me_b],
            device_id={"blk": peer},
            device_id_type=MESH,
        )
        copy.start()
        landing = pltpu.make_async_remote_copy(
            src_ref=gath.at[peer],
            dst_ref=gath.at[peer],
            send_sem=gs_sem.at[s],
            recv_sem=gr_sem.at[peer],
            device_id={"blk": peer},
            device_id_type=MESH,
        )
        gathers.append((copy, landing))

    w_kv = nn(loaded("sel_kv")[...], loaded("w_kv")[...]).astype(bf16)
    w_kp = nn(loaded("sel_kp")[...], loaded("w_kp")[...]).astype(bf16)
    w_qp = nn(loaded("sel_q")[...], loaded("w_qp")[...]).astype(bf16)
    query = nt(single, loaded("w_q")[...]) * (1.0 / math.sqrt(size))
    q_local = nt(w_qp, single)
    step = queries * SUB

    def moved(local, base, count, turn):
        out = []
        for a in range(3):
            total = turn[9 + a : 10 + a]
            mixed = sum(
                turn[3 * a + b : 3 * a + b + 1] * local[base + b * count : base + (b + 1) * count]
                for b in range(3)
            )
            out.append(mixed + total)
        return out

    q_global = moved(q_local, 0, step, frames)
    for a in range(3):
        for p in range(queries):
            for i in range(rows):
                spot = ((a * queries + p) * rows + i) * SUB
                qb[spot : spot + SUB, :] = jnp.broadcast_to(
                    q_global[a][p * SUB : (p + 1) * SUB, i : i + 1], (SUB, LANES)
                )

    def along_keys(value):
        if keys <= LANES:
            return value[:, :keys]
        return jnp.concatenate([value] * (keys // LANES), axis=1)

    eye = (
        lax.broadcasted_iota(jnp.int32, (SUB, heads), 0)
        == lax.broadcasted_iota(jnp.int32, (SUB, heads), 1)
    ).astype(bf16)
    w_bias = nn(eye, loaded("w_bias")[...]).astype(bf16)
    wbb_ref = loaded("w_back")
    eye6 = (
        lax.broadcasted_iota(jnp.int32, (SUB, wbb_ref.shape[0]), 0)
        == lax.broadcasted_iota(jnp.int32, (SUB, wbb_ref.shape[0]), 1)
    ).astype(bf16)
    w_back = nn(eye6, wbb_ref[...]).astype(bf16)
    head_row = lax.broadcasted_iota(jnp.int32, (SUB, keys), 0)
    raw = jnp.zeros((SUB, keys), f32)
    chain_term = jnp.zeros((SUB, keys), f32)
    hw_ref, cb_ref = loaded("head_weights"), loaded("chain_bias")
    for h in range(heads):
        raw = jnp.where(head_row == h, hw_ref[h], raw)
        chain_term = jnp.where(head_row == h, cb_ref[h], chain_term)
    soft = jnp.maximum(raw, 0.0) + jnp.log1p(jnp.exp(-jnp.abs(raw)))
    distance_scale = soft * (math.sqrt(2.0 / (9.0 * queries)) / 2.0)
    own_head = (
        lax.broadcasted_iota(jnp.int32, (SUB, heads * size), 1) // size
        == lax.broadcasted_iota(jnp.int32, (SUB, heads * size), 0)
    ).astype(f32)
    q_wide = (query[:, None, :] * own_head[None]).reshape(rows * SUB, heads * size)
    pair_v = loaded("pair")
    pairs = [pair_v[i * keys : (i + 1) * keys, :] for i in range(rows)]
    biases = [nt(w_bias, pairs[i]) for i in range(rows)]
    wout_v = loaded("w_out")
    small = size + 4 * values
    w_small = nn(
        loaded("sel_out")[...], jnp.concatenate([wout_v[h, :small, :] for h in range(heads)], axis=0)
    ).astype(bf16)

    for copy, landing in gathers:
        landing.wait_recv()
    everyone = gath[...].reshape(keys, width + LANES)
    key_single = everyone[:, :width].astype(bf16)
    key_meta = everyone[:, width:].T
    kv = nt(w_kv, key_single)
    key_rows = up(heads * size, 16)
    kp = nt(w_kp, key_single)
    k_global = moved(kp, 0, step, key_meta)
    v_global = moved(kp, 3 * step, wide, key_meta)
    dots = dot3(nn, q_wide, kv[: heads * size])
    key_chain = jnp.broadcast_to(key_meta[12:13], (SUB, keys))
    key_present = jnp.broadcast_to(key_meta[13:14], (SUB, keys))
    chain_ref, mask_ref = loaded("chain"), loaded("mask")

    weights, tops, totals = [], [], []
    for i in range(rows):
        distance = jnp.zeros((SUB, keys), f32)
        for a in range(3):
            for p in range(queries):
                spot = ((a * queries + p) * rows + i) * SUB
                gap = along_keys(qb[spot : spot + SUB, :]) - k_global[a][p * SUB : (p + 1) * SUB, :]
                distance = distance + gap * gap
        differ = jnp.where(key_chain != chain_ref[i].astype(f32), chain_term, 0.0)
        logits = LOGIT_WEIGHT * (
            dots[i * SUB : (i + 1) * SUB] + biases[i] - distance_scale * distance + differ
        )
        absent = 1.0 - mask_ref[i].astype(f32) * key_present
        logits = logits - MASK_PENALTY * absent
        top = jnp.max(logits, axis=1, keepdims=True)
        weight = jnp.exp(logits - top)
        weights.append(weight)
        tops.append(jnp.broadcast_to(top, (SUB, LANES)))
        totals.append(jnp.broadcast_to(jnp.sum(weight, axis=1, keepdims=True), (SUB, LANES)))

    lane = lax.broadcasted_iota(jnp.int32, (SUB, LANES), 1)
    row = lax.broadcasted_iota(jnp.int32, (SUB, LANES), 0)
    stat = jnp.concatenate(
        [
            jnp.sum(
                jnp.where(lane == row, tops[i], jnp.where(lane == row + SUB, totals[i], 0.0)),
                axis=0,
                keepdims=True,
            )
            for i in range(rows)
        ],
        axis=0,
    )
    wide_lane = lax.broadcasted_iota(jnp.int32, (SUB, wide), 1)
    wide_row = lax.broadcasted_iota(jnp.int32, (SUB, wide), 0)
    keep_value = (wide_lane // size == wide_row).astype(f32)
    keep_point = (wide_lane // values == wide_row).astype(f32)
    keep = jnp.concatenate([keep_value, keep_point, keep_point, keep_point], axis=1)
    every = jnp.concatenate(weights, axis=0)
    sums = dot3(nt, every, jnp.concatenate([kv[key_rows:]] + v_global, axis=0))
    sums = jnp.sum(sums.reshape(rows, SUB, 4 * wide) * keep[None], axis=1)
    ex[0, :, :LANES] = stat
    ex[0, :, LANES:] = sums[:, wide:]
    exchanges = []
    for d in range(1, npr):
        copy = pltpu.make_async_remote_copy(
            src_ref=ex.at[0],
            dst_ref=ex.at[d],
            send_sem=es_sem.at[d],
            recv_sem=er_sem.at[d],
            device_id=group_peer(0, d),
            device_id_type=MESH,
        )
        copy.start()
        exchanges.append(copy)

    for i in range(rows):
        sp[i * SUB : (i + 1) * SUB, :] = nn(weights[i].astype(bf16), pairs[i])

    for copy in exchanges:
        copy.wait()
    stats = [stat] + [ex[d, :, :LANES] for d in range(1, npr)]
    best = functools.reduce(jnp.maximum, [s[:, :SUB] for s in stats])
    scales = [jnp.exp(s[:, :SUB] - best) for s in stats]
    total = sum(s[:, SUB : 2 * SUB] * scale for s, scale in zip(stats, scales))
    factors = [scale / total for scale in scales]
    full_lane = lax.broadcasted_iota(jnp.int32, (rows, wide), 1)

    def spread(factor, count):
        out = jnp.zeros((rows, wide), f32)
        for h in range(heads):
            out = jnp.where(full_lane // count == h, factor[:, h : h + 1], out)
        return out

    attended = sums[:, :wide] * spread(factors[0], size)
    pointed_global = []
    for a in range(3):
        pointed_global.append(sums[:, (1 + a) * wide : (2 + a) * wide] * spread(factors[0], values))
    for d in range(1, npr):
        scale = spread(factors[d], values)
        for a in range(3):
            base = LANES + a * wide
            pointed_global[a] = pointed_global[a] + ex[d, :, base : base + wide] * scale
    shifted = [pointed_global[a] - meta[:, 9 + a : 10 + a] for a in range(3)]
    pointed = [
        sum(meta[:, 3 * a + b : 3 * a + b + 1] * shifted[a] for a in range(3)) for b in range(3)
    ]
    norms = jnp.sqrt(sum(p * p for p in pointed) + 1.0)
    features = [attended] + [p * (1.0 / npr) for p in pointed + [norms]]
    partial = sum(
        nn(feature.astype(bf16), w_small[k * wide : (k + 1) * wide])
        for k, feature in enumerate(features)
    )
    for h in range(heads):
        paired = sp[pl.ds(h, rows, stride=SUB), :] * factors[0][:, h : h + 1]
        partial = partial + nn(paired.astype(bf16), wout_v[h, small:, :])
    part[...] = partial
    reductions = []
    for dh, dp in group:
        code = dh * npr + dp
        target = pl.multiple_of(lax.rem(me_p + dp, npr) * half, half)
        copy = pltpu.make_async_remote_copy(
            src_ref=part.at[pl.ds(target, half)],
            dst_ref=red.at[code],
            send_sem=rs_sem.at[code],
            recv_sem=rr_sem.at[code],
            device_id=group_peer(dh, dp),
            device_id_type=MESH,
        )
        copy.start()
        reductions.append(copy)
    red[0] = part[pl.ds(start, half), :]
    for copy, landing in gathers:
        copy.wait_send()
    for copy in reductions:
        copy.wait()
    update = jnp.zeros((half, width), f32)
    for h in range(nh):
        for p in range(npr):
            code = lax.rem(me_h - h + nh, nh) * npr + lax.rem(me_p - p + npr, npr)
            update = update + red[code]
    mixed = gath[me_b, :, :width] + update
    centre = jnp.mean(mixed, axis=1, keepdims=True)
    away = mixed - centre
    variance = jnp.mean(away * away, axis=1, keepdims=True)
    out = (away * lax.rsqrt(variance + 1e-05) * loaded("gain")[...].reshape(1, width)).astype(bf16)
    motion = nt(w_back, out)
    m = [motion[k : k + 1] for k in range(6)]
    inverse = 1.0 / jnp.sqrt(1.0 + m[0] * m[0] + m[1] * m[1] + m[2] * m[2])
    qa, qb, qc, qd = inverse, m[0] * inverse, m[1] * inverse, m[2] * inverse
    spin = [
        qa * qa + qb * qb - qc * qc - qd * qd,
        2.0 * (qb * qc - qa * qd),
        2.0 * (qb * qd + qa * qc),
        2.0 * (qb * qc + qa * qd),
        qa * qa - qb * qb + qc * qc - qd * qd,
        2.0 * (qc * qd - qa * qb),
        2.0 * (qb * qd - qa * qc),
        2.0 * (qc * qd + qa * qb),
        qa * qa - qb * qb - qc * qc + qd * qd,
    ]
    turn = [my_frames[k : k + 1] for k in range(12)]
    lines = [
        sum(turn[3 * a + b] * spin[3 * b + c] for b in range(3)) for a in range(3) for c in range(3)
    ]
    lines += [
        turn[9 + a] + sum(turn[3 * a + b] * m[3 + b] for b in range(3)) for a in range(3)
    ]
    lines = jnp.concatenate(lines + [jnp.zeros((4, half), f32)], axis=0)
    fg[...] = jnp.concatenate([lines, jnp.zeros((16, LANES - half), f32)], axis=1)
    finals = []
    for d, dp in block:
        code = d * npr + dp
        copy = pltpu.make_async_remote_copy(
            src_ref=fg,
            dst_ref=fo_ref.at[me_b, me_p],
            send_sem=fs_sem.at[code],
            recv_sem=fr_sem.at[code],
            device_id=block_peer(d, dp),
            device_id_type=MESH,
        )
        copy.start()
        finals.append(copy)
    so32[...] = out.astype(f32)
    for d in range(1, npr):
        copy = pltpu.make_async_remote_copy(
            src_ref=so32,
            dst_ref=so_ref.at[me_p],
            send_sem=os_sem.at[d],
            recv_sem=or_sem.at[d],
            device_id=group_peer(0, d),
            device_id_type=MESH,
        )
        copy.start()
        finals.append(copy)
    for source, target, slot in ((fg, fo_ref.at[me_b, me_p], fs_sem), (so32, so_ref.at[me_p], os_sem)):
        copy = pltpu.make_async_copy(source, target, slot.at[0])
        copy.start()
        finals.append(copy)
    for copy in finals:
        copy.wait()


def finish(halves_ref, pieces_ref, so_ref, fo_ref):
    parts, half = halves_ref.shape[:2]
    for p in range(parts):
        so_ref[p * half : (p + 1) * half, :] = halves_ref[p].astype(jnp.bfloat16)
    for k in range(pieces_ref.shape[0]):
        for p in range(parts):
            spot = (k * parts + p) * half
            fo_ref[:, spot : spot + half] = pieces_ref[k, p, :12, :half]


def body(
    single, pair, frames, chain, mask, w_query, w_key_value, w_query_points, w_kv_points,
    w_pair_bias, head_weights, chain_bias, w_out, out_gain, w_backbone,
):
    nb, nh, npr = (lax.axis_size(a) for a in ("blk", "head", "pair"))
    rows, width = single.shape
    half = rows // npr
    channels = pair.shape[3]
    heads = w_pair_bias.shape[1]
    size = w_query.shape[1] // heads
    queries = w_query_points.shape[1] // (3 * heads)
    values = w_kv_points.shape[1] // (3 * heads) - queries
    wide = up(heads * max(size, values), LANES)
    dims = (nb, nh, npr, heads, size, queries, values)
    vmem = pl.BlockSpec(memory_space=pltpu.VMEM)
    dma = pltpu.SemaphoreType.DMA
    selected = selectors(heads, size, queries, values)
    given = dict(zip(("sel_q", "sel_kv", "sel_kp", "sel_out"), selected))
    given.update(
        single=single, pair=pair.reshape(rows * nb * half, channels), frames=frames,
        chain_row=chain.reshape(1, rows), mask_row=mask.reshape(1, rows), chain=chain, mask=mask,
        w_q=w_query.T, w_kv=w_key_value.T, w_qp=w_query_points.T, w_kp=w_kv_points.T,
        w_bias=w_pair_bias.T, head_weights=head_weights, chain_bias=chain_bias, w_out=w_out,
        gain=out_gain, w_back=w_backbone.T,
    )
    operands = [given[name] for name in ORDER]
    held = [
        (pltpu.SMEM if name in SCALARS else pltpu.VMEM)(given[name].shape, given[name].dtype)
        for name in ORDER
    ]
    far = pl.BlockSpec(memory_space=pl.ANY)
    pieces = pl.pallas_call(
        functools.partial(kernel, dims),
        out_shape=(
            jax.ShapeDtypeStruct((npr, half, width), jnp.float32),
            jax.ShapeDtypeStruct((nb, npr, 16, LANES), jnp.float32),
        ),
        in_specs=[far] * len(operands),
        out_specs=(far, far),
        scratch_shapes=held
        + [
            pltpu.VMEM((nb, half, width + LANES), jnp.float32),
            pltpu.VMEM((rows, LANES), jnp.float32),
            pltpu.VMEM((3 * queries * rows * SUB, LANES), jnp.float32),
            pltpu.VMEM((rows * SUB, channels), jnp.float32),
            pltpu.VMEM((npr, rows, LANES + 3 * wide), jnp.float32),
            pltpu.VMEM((rows, width), jnp.float32),
            pltpu.VMEM((nh * npr, half, width), jnp.float32),
            pltpu.VMEM((half, width), jnp.float32),
            pltpu.VMEM((16, LANES), jnp.float32),
            dma((len(operands),)),
            dma((nb,)),
            dma((nb,)),
            dma((npr,)),
            dma((npr,)),
            dma((nh * npr,)),
            dma((nh * npr,)),
            dma((nb * npr,)),
            dma((nb * npr,)),
            dma((npr,)),
            dma((npr,)),
        ],
        compiler_params=pltpu.CompilerParams(collective_id=0, has_side_effects=True),
    )(*operands)
    return tuple(
        pl.pallas_call(
            finish,
            out_shape=(
                jax.ShapeDtypeStruct((rows, width), jnp.bfloat16),
                jax.ShapeDtypeStruct((12, nb * rows), jnp.float32),
            ),
            in_specs=[vmem, vmem],
            out_specs=(vmem, vmem),
        )(*pieces)
    )


def solution(mesh):
    placed = (
        P(("groups", "blk"), None),
        P(("groups", "blk"), None, "pair", None),
        P(None, ("groups", "blk")),
        P(("groups", "blk")),
        P(("groups", "blk")),
        P(None, "head"),
        P(None, "head"),
        P(None, "head"),
        P(None, "head"),
        P(None, "head"),
        P("head"),
        P("head"),
        P("head", None, None),
        P(),
        P(),
    )
    return jax.shard_map(
        body,
        mesh=mesh,
        in_specs=placed,
        out_specs=(P(("groups", "blk"), None), P(None, "groups")),
        check_vma=False,
    )
```

```python
import functools
import math

import jax
import jax.numpy as jnp
import numpy as np
from jax import lax
from jax.experimental import pallas as pl
from jax.experimental.pallas import tpu as pltpu
from jax.sharding import PartitionSpec as P

LOGIT_WEIGHT = math.sqrt(1.0 / 3.0)
MASK_PENALTY = 100000.0
MESH = pl.DeviceIdType.MESH
LANES = 128
SUB = 8


def up(value, unit):
    return -(-value // unit) * unit


def nt(a, b):
    return lax.dot_general(a, b, (((1,), (1,)), ((), ())), preferred_element_type=jnp.float32)


def nn(a, b):
    return lax.dot_general(a, b, (((1,), (0,)), ((), ())), preferred_element_type=jnp.float32)


def halves(value):
    high = value.astype(jnp.bfloat16)
    return high, (value - high.astype(jnp.float32)).astype(jnp.bfloat16)


def dot3(product, a, b):
    a_high, a_low = halves(a)
    b_high, b_low = halves(b)
    return product(a_high, b_high) + (product(a_low, b_high) + product(a_high, b_low))


def selectors(heads, size, queries, values):
    wide = up(heads * max(size, values), LANES)
    sel_q = np.zeros((3 * queries * SUB, heads * queries * 3), np.float32)
    key_rows = up(heads * size, 16)
    sel_kv = np.zeros((key_rows + wide, heads * 2 * size), np.float32)
    sel_kp = np.zeros((3 * queries * SUB + 3 * wide, heads * (queries + values) * 3), np.float32)
    small = size + 4 * values
    sel_out = np.zeros((5 * wide, heads * small), np.float32)
    for h in range(heads):
        for b in range(3):
            for p in range(queries):
                row = (b * queries + p) * SUB + h
                sel_q[row, (h * queries + p) * 3 + b] = 1
                sel_kp[row, (h * (queries + values) + p) * 3 + b] = 1
            for p in range(values):
                row = 3 * queries * SUB + b * wide + h * values + p
                sel_kp[row, (h * (queries + values) + queries + p) * 3 + b] = 1
                sel_out[(1 + b) * wide + h * values + p, h * small + size + p * 3 + b] = 1
        for p in range(values):
            sel_out[4 * wide + h * values + p, h * small + size + 3 * values + p] = 1
        for c in range(size):
            sel_kv[h * size + c, h * 2 * size + c] = 1
            sel_kv[key_rows + h * size + c, h * 2 * size + size + c] = 1
            sel_out[h * size + c, h * small + c] = 1
    return [jnp.asarray(s, jnp.bfloat16) for s in (sel_q, sel_kv, sel_kp, sel_out)]


ORDER = (
    "frames", "chain_row", "mask_row", "single", "sel_kv", "w_kv", "sel_kp", "w_kp", "sel_q", "w_qp",
    "w_q", "w_bias", "w_back", "head_weights", "chain_bias", "pair", "w_out", "sel_out", "chain",
    "mask", "gain",
)
SCALARS = ("head_weights", "chain_bias", "chain", "mask")


def kernel(dims, *refs):
    count = len(ORDER)
    far = refs[:count]
    so_ref, fo_ref = refs[count : count + 2]
    near = dict(zip(ORDER, refs[count + 2 : 2 * count + 2]))
    (
        gath, meta_s, qb, sp, ex, part, red, so32, fg,
        load_sem, gs_sem, gr_sem, es_sem, er_sem, rs_sem, rr_sem, fs_sem, fr_sem,
        os_sem, or_sem,
    ) = refs[2 * count + 2 :]
    loads = {
        name: pltpu.make_async_copy(source, near[name], load_sem.at[k])
        for k, (name, source) in enumerate(zip(ORDER, far))
    }

    def loaded(name):
        loads[name].wait()
        return near[name]

    nb, nh, npr, heads, size, queries, values = dims
    rows, width = near["single"].shape
    half = rows // npr
    keys = nb * half
    wide = up(heads * max(size, values), LANES)
    me_b = lax.axis_index("blk")
    me_h = lax.axis_index("head")
    me_p = lax.axis_index("pair")
    f32, bf16 = jnp.float32, jnp.bfloat16

    def block_peer(d, dp):
        return {"blk": lax.rem(me_b + d, nb), "pair": lax.rem(me_p + dp, npr)}

    def group_peer(dh, dp):
        return {"head": lax.rem(me_h + dh, nh), "pair": lax.rem(me_p + dp, npr)}

    block = [(d, dp) for d in range(nb) for dp in range(npr) if d or dp]
    group = [(dh, dp) for dh in range(nh) for dp in range(npr) if dh or dp]
    barrier = pltpu.get_barrier_semaphore()
    for peer in [block_peer(d, dp) for d, dp in block] + [group_peer(dh, dp) for dh, dp in group if dh]:
        pl.semaphore_signal(barrier, inc=1, device_id=peer, device_id_type=MESH)
    for name in ORDER:
        loads[name].start()
    frames = loaded("frames")[...]
    chain_row = loaded("chain_row")[...].astype(f32)
    mask_row = loaded("mask_row")[...].astype(f32)
    single_ref = loaded("single")
    meta = jnp.concatenate(
        [
            frames,
            chain_row,
            mask_row,
            jnp.zeros((LANES - 14, rows), f32),
        ],
        axis=0,
    ).T
    meta_s[...] = meta
    start = pl.multiple_of(me_p * half, half)
    gath[me_b, :, :width] = single_ref[pl.ds(start, half), :].astype(f32)
    gath[me_b, :, width:] = meta_s[pl.ds(start, half), :]
    my_frames = meta_s[pl.ds(start, half), :].T

    single = single_ref[...]
    pl.semaphore_wait(barrier, len(block) + (nh - 1) * npr)
    gathers = []
    upper = (2 * me_b) // nb
    for s in range(nb - 1):
        rising = s + (s - me_b + nb) // nb
        falling = nb - 1 - s - (me_b - (nb - 1 - s) + nb) // nb
        peer = upper * rising + (1 - upper) * falling
        copy = pltpu.make_async_remote_copy(
            src_ref=gath.at[me_b],
            dst_ref=gath.at[me_b],
            send_sem=gs_sem.at[s],
            recv_sem=gr_sem.at[me_b],
            device_id={"blk": peer},
            device_id_type=MESH,
        )
        copy.start()
        landing = pltpu.make_async_remote_copy(
            src_ref=gath.at[peer],
            dst_ref=gath.at[peer],
            send_sem=gs_sem.at[s],
            recv_sem=gr_sem.at[peer],
            device_id={"blk": peer},
            device_id_type=MESH,
        )
        gathers.append((copy, landing))

    w_kv = nn(loaded("sel_kv")[...], loaded("w_kv")[...]).astype(bf16)
    w_kp = nn(loaded("sel_kp")[...], loaded("w_kp")[...]).astype(bf16)
    w_qp = nn(loaded("sel_q")[...], loaded("w_qp")[...]).astype(bf16)
    query = nt(single, loaded("w_q")[...]) * (1.0 / math.sqrt(size))
    q_local = nt(w_qp, single)
    step = queries * SUB

    def moved(local, base, count, turn):
        out = []
        for a in range(3):
            total = turn[9 + a : 10 + a]
            mixed = sum(
                turn[3 * a + b : 3 * a + b + 1] * local[base + b * count : base + (b + 1) * count]
                for b in range(3)
            )
            out.append(mixed + total)
        return out

    q_global = moved(q_local, 0, step, frames)
    for a in range(3):
        for p in range(queries):
            for i in range(rows):
                spot = ((a * queries + p) * rows + i) * SUB
                qb[spot : spot + SUB, :] = jnp.broadcast_to(
                    q_global[a][p * SUB : (p + 1) * SUB, i : i + 1], (SUB, LANES)
                )

    def along_keys(value):
        if keys <= LANES:
            return value[:, :keys]
        return jnp.concatenate([value] * (keys // LANES), axis=1)

    eye = (
        lax.broadcasted_iota(jnp.int32, (SUB, heads), 0)
        == lax.broadcasted_iota(jnp.int32, (SUB, heads), 1)
    ).astype(bf16)
    w_bias = nn(eye, loaded("w_bias")[...]).astype(bf16)
    wbb_ref = loaded("w_back")
    eye6 = (
        lax.broadcasted_iota(jnp.int32, (SUB, wbb_ref.shape[0]), 0)
        == lax.broadcasted_iota(jnp.int32, (SUB, wbb_ref.shape[0]), 1)
    ).astype(bf16)
    w_back = nn(eye6, wbb_ref[...]).astype(bf16)
    head_row = lax.broadcasted_iota(jnp.int32, (SUB, keys), 0)
    raw = jnp.zeros((SUB, keys), f32)
    chain_term = jnp.zeros((SUB, keys), f32)
    hw_ref, cb_ref = loaded("head_weights"), loaded("chain_bias")
    for h in range(heads):
        raw = jnp.where(head_row == h, hw_ref[h], raw)
        chain_term = jnp.where(head_row == h, cb_ref[h], chain_term)
    soft = jnp.maximum(raw, 0.0) + jnp.log1p(jnp.exp(-jnp.abs(raw)))
    distance_scale = soft * (math.sqrt(2.0 / (9.0 * queries)) / 2.0)
    own_head = (
        lax.broadcasted_iota(jnp.int32, (SUB, heads * size), 1) // size
        == lax.broadcasted_iota(jnp.int32, (SUB, heads * size), 0)
    ).astype(f32)
    q_wide = (query[:, None, :] * own_head[None]).reshape(rows * SUB, heads * size)
    pair_v = loaded("pair")
    pairs = [pair_v[i * keys : (i + 1) * keys, :] for i in range(rows)]
    biases = [nt(w_bias, pairs[i]) for i in range(rows)]
    wout_v = loaded("w_out")
    small = size + 4 * values
    w_small = nn(
        loaded("sel_out")[...], jnp.concatenate([wout_v[h, :small, :] for h in range(heads)], axis=0)
    ).astype(bf16)

    for copy, landing in gathers:
        landing.wait_recv()
    everyone = gath[...].reshape(keys, width + LANES)
    key_single = everyone[:, :width].astype(bf16)
    key_meta = everyone[:, width:].T
    kv = nt(w_kv, key_single)
    key_rows = up(heads * size, 16)
    kp = nt(w_kp, key_single)
    k_global = moved(kp, 0, step, key_meta)
    v_global = moved(kp, 3 * step, wide, key_meta)
    dots = dot3(nn, q_wide, kv[: heads * size])
    key_chain = jnp.broadcast_to(key_meta[12:13], (SUB, keys))
    key_present = jnp.broadcast_to(key_meta[13:14], (SUB, keys))
    chain_ref, mask_ref = loaded("chain"), loaded("mask")

    weights, tops, totals = [], [], []
    for i in range(rows):
        distance = jnp.zeros((SUB, keys), f32)
        for a in range(3):
            for p in range(queries):
                spot = ((a * queries + p) * rows + i) * SUB
                gap = along_keys(qb[spot : spot + SUB, :]) - k_global[a][p * SUB : (p + 1) * SUB, :]
                distance = distance + gap * gap
        differ = jnp.where(key_chain != chain_ref[i].astype(f32), chain_term, 0.0)
        logits = LOGIT_WEIGHT * (
            dots[i * SUB : (i + 1) * SUB] + biases[i] - distance_scale * distance + differ
        )
        absent = 1.0 - mask_ref[i].astype(f32) * key_present
        logits = logits - MASK_PENALTY * absent
        top = jnp.max(logits, axis=1, keepdims=True)
        weight = jnp.exp(logits - top)
        weights.append(weight)
        tops.append(jnp.broadcast_to(top, (SUB, LANES)))
        totals.append(jnp.broadcast_to(jnp.sum(weight, axis=1, keepdims=True), (SUB, LANES)))

    lane = lax.broadcasted_iota(jnp.int32, (SUB, LANES), 1)
    row = lax.broadcasted_iota(jnp.int32, (SUB, LANES), 0)
    stat = jnp.concatenate(
        [
            jnp.sum(
                jnp.where(lane == row, tops[i], jnp.where(lane == row + SUB, totals[i], 0.0)),
                axis=0,
                keepdims=True,
            )
            for i in range(rows)
        ],
        axis=0,
    )
    wide_lane = lax.broadcasted_iota(jnp.int32, (SUB, wide), 1)
    wide_row = lax.broadcasted_iota(jnp.int32, (SUB, wide), 0)
    keep_value = (wide_lane // size == wide_row).astype(f32)
    keep_point = (wide_lane // values == wide_row).astype(f32)
    keep = jnp.concatenate([keep_value, keep_point, keep_point, keep_point], axis=1)
    every = jnp.concatenate(weights, axis=0)
    sums = dot3(nt, every, jnp.concatenate([kv[key_rows:]] + v_global, axis=0))
    sums = jnp.sum(sums.reshape(rows, SUB, 4 * wide) * keep[None], axis=1)
    ex[0, :, :LANES] = stat
    ex[0, :, LANES:] = sums[:, wide:]
    exchanges = []
    for d in range(1, npr):
        copy = pltpu.make_async_remote_copy(
            src_ref=ex.at[0],
            dst_ref=ex.at[d],
            send_sem=es_sem.at[d],
            recv_sem=er_sem.at[d],
            device_id=group_peer(0, d),
            device_id_type=MESH,
        )
        copy.start()
        exchanges.append(copy)

    for i in range(rows):
        sp[i * SUB : (i + 1) * SUB, :] = nn(weights[i].astype(bf16), pairs[i])

    for copy in exchanges:
        copy.wait()
    stats = [stat] + [ex[d, :, :LANES] for d in range(1, npr)]
    best = functools.reduce(jnp.maximum, [s[:, :SUB] for s in stats])
    scales = [jnp.exp(s[:, :SUB] - best) for s in stats]
    total = sum(s[:, SUB : 2 * SUB] * scale for s, scale in zip(stats, scales))
    factors = [scale / total for scale in scales]
    full_lane = lax.broadcasted_iota(jnp.int32, (rows, wide), 1)

    def spread(factor, count):
        out = jnp.zeros((rows, wide), f32)
        for h in range(heads):
            out = jnp.where(full_lane // count == h, factor[:, h : h + 1], out)
        return out

    attended = sums[:, :wide] * spread(factors[0], size)
    pointed_global = []
    for a in range(3):
        pointed_global.append(sums[:, (1 + a) * wide : (2 + a) * wide] * spread(factors[0], values))
    for d in range(1, npr):
        scale = spread(factors[d], values)
        for a in range(3):
            base = LANES + a * wide
            pointed_global[a] = pointed_global[a] + ex[d, :, base : base + wide] * scale
    shifted = [pointed_global[a] - meta[:, 9 + a : 10 + a] for a in range(3)]
    pointed = [
        sum(meta[:, 3 * a + b : 3 * a + b + 1] * shifted[a] for a in range(3)) for b in range(3)
    ]
    norms = jnp.sqrt(sum(p * p for p in pointed) + 1.0)
    features = [attended] + [p * (1.0 / npr) for p in pointed + [norms]]
    features = [feature.astype(bf16) for feature in features]
    paired = [
        (sp[pl.ds(h, rows, stride=SUB), :] * factors[0][:, h : h + 1]).astype(bf16)
        for h in range(heads)
    ]
    cuts = [slice(k, min(k + 2 * LANES, width)) for k in range(0, width, 2 * LANES)]
    reductions = []
    for number, columns in enumerate(cuts):
        partial = sum(
            nn(feature, w_small[k * wide : (k + 1) * wide, columns])
            for k, feature in enumerate(features)
        )
        for h in range(heads):
            partial = partial + nn(paired[h], wout_v[h, small:, columns])
        part[:, columns] = partial
        for dh, dp in reversed(group):
            code = dh * npr + dp
            target = pl.multiple_of(lax.rem(me_p + dp, npr) * half, half)
            copy = pltpu.make_async_remote_copy(
                src_ref=part.at[pl.ds(target, half), columns],
                dst_ref=red.at[code, :, columns],
                send_sem=rs_sem.at[number, code],
                recv_sem=rr_sem.at[number, code],
                device_id=group_peer(dh, dp),
                device_id_type=MESH,
            )
            copy.start()
            reductions.append(copy)
    red[0] = part[pl.ds(start, half), :]
    for copy, landing in gathers:
        copy.wait_send()
    for copy in reductions:
        copy.wait()
    update = jnp.zeros((half, width), f32)
    for h in range(nh):
        for p in range(npr):
            code = lax.rem(me_h - h + nh, nh) * npr + lax.rem(me_p - p + npr, npr)
            update = update + red[code]
    mixed = gath[me_b, :, :width] + update
    centre = jnp.mean(mixed, axis=1, keepdims=True)
    away = mixed - centre
    variance = jnp.mean(away * away, axis=1, keepdims=True)
    out = (away * lax.rsqrt(variance + 1e-05) * loaded("gain")[...].reshape(1, width)).astype(bf16)
    motion = nt(w_back, out)
    m = [motion[k : k + 1] for k in range(6)]
    inverse = 1.0 / jnp.sqrt(1.0 + m[0] * m[0] + m[1] * m[1] + m[2] * m[2])
    qa, qb, qc, qd = inverse, m[0] * inverse, m[1] * inverse, m[2] * inverse
    spin = [
        qa * qa + qb * qb - qc * qc - qd * qd,
        2.0 * (qb * qc - qa * qd),
        2.0 * (qb * qd + qa * qc),
        2.0 * (qb * qc + qa * qd),
        qa * qa - qb * qb + qc * qc - qd * qd,
        2.0 * (qc * qd - qa * qb),
        2.0 * (qb * qd - qa * qc),
        2.0 * (qc * qd + qa * qb),
        qa * qa - qb * qb - qc * qc + qd * qd,
    ]
    turn = [my_frames[k : k + 1] for k in range(12)]
    lines = [
        sum(turn[3 * a + b] * spin[3 * b + c] for b in range(3)) for a in range(3) for c in range(3)
    ]
    lines += [
        turn[9 + a] + sum(turn[3 * a + b] * m[3 + b] for b in range(3)) for a in range(3)
    ]
    lines = jnp.concatenate(lines + [jnp.zeros((4, half), f32)], axis=0)
    fg[...] = jnp.concatenate([lines, jnp.zeros((16, LANES - half), f32)], axis=1)
    finals = []
    for d, dp in block:
        code = d * npr + dp
        copy = pltpu.make_async_remote_copy(
            src_ref=fg,
            dst_ref=fo_ref.at[me_b, me_p],
            send_sem=fs_sem.at[code],
            recv_sem=fr_sem.at[code],
            device_id=block_peer(d, dp),
            device_id_type=MESH,
        )
        copy.start()
        finals.append(copy)
    so32[...] = out.astype(f32)
    for d in range(1, npr):
        copy = pltpu.make_async_remote_copy(
            src_ref=so32,
            dst_ref=so_ref.at[me_p],
            send_sem=os_sem.at[d],
            recv_sem=or_sem.at[d],
            device_id=group_peer(0, d),
            device_id_type=MESH,
        )
        copy.start()
        finals.append(copy)
    for source, target, slot in ((fg, fo_ref.at[me_b, me_p], fs_sem), (so32, so_ref.at[me_p], os_sem)):
        copy = pltpu.make_async_copy(source, target, slot.at[0])
        copy.start()
        finals.append(copy)
    for copy in finals:
        copy.wait()


def finish(halves_ref, pieces_ref, so_ref, fo_ref):
    parts, half = halves_ref.shape[:2]
    for p in range(parts):
        so_ref[p * half : (p + 1) * half, :] = halves_ref[p].astype(jnp.bfloat16)
    for k in range(pieces_ref.shape[0]):
        for p in range(parts):
            spot = (k * parts + p) * half
            fo_ref[:, spot : spot + half] = pieces_ref[k, p, :12, :half]


def body(
    single, pair, frames, chain, mask, w_query, w_key_value, w_query_points, w_kv_points,
    w_pair_bias, head_weights, chain_bias, w_out, out_gain, w_backbone,
):
    nb, nh, npr = (lax.axis_size(a) for a in ("blk", "head", "pair"))
    rows, width = single.shape
    half = rows // npr
    channels = pair.shape[3]
    heads = w_pair_bias.shape[1]
    size = w_query.shape[1] // heads
    queries = w_query_points.shape[1] // (3 * heads)
    values = w_kv_points.shape[1] // (3 * heads) - queries
    wide = up(heads * max(size, values), LANES)
    dims = (nb, nh, npr, heads, size, queries, values)
    vmem = pl.BlockSpec(memory_space=pltpu.VMEM)
    dma = pltpu.SemaphoreType.DMA
    selected = selectors(heads, size, queries, values)
    given = dict(zip(("sel_q", "sel_kv", "sel_kp", "sel_out"), selected))
    given.update(
        single=single, pair=pair.reshape(rows * nb * half, channels), frames=frames,
        chain_row=chain.reshape(1, rows), mask_row=mask.reshape(1, rows), chain=chain, mask=mask,
        w_q=w_query.T, w_kv=w_key_value.T, w_qp=w_query_points.T, w_kp=w_kv_points.T,
        w_bias=w_pair_bias.T, head_weights=head_weights, chain_bias=chain_bias, w_out=w_out,
        gain=out_gain, w_back=w_backbone.T,
    )
    operands = [given[name] for name in ORDER]
    held = [
        (pltpu.SMEM if name in SCALARS else pltpu.VMEM)(given[name].shape, given[name].dtype)
        for name in ORDER
    ]
    far = pl.BlockSpec(memory_space=pl.ANY)
    pieces = pl.pallas_call(
        functools.partial(kernel, dims),
        out_shape=(
            jax.ShapeDtypeStruct((npr, half, width), jnp.float32),
            jax.ShapeDtypeStruct((nb, npr, 16, LANES), jnp.float32),
        ),
        in_specs=[far] * len(operands),
        out_specs=(far, far),
        scratch_shapes=held
        + [
            pltpu.VMEM((nb, half, width + LANES), jnp.float32),
            pltpu.VMEM((rows, LANES), jnp.float32),
            pltpu.VMEM((3 * queries * rows * SUB, LANES), jnp.float32),
            pltpu.VMEM((rows * SUB, channels), jnp.float32),
            pltpu.VMEM((npr, rows, LANES + 3 * wide), jnp.float32),
            pltpu.VMEM((rows, width), jnp.float32),
            pltpu.VMEM((nh * npr, half, width), jnp.float32),
            pltpu.VMEM((half, width), jnp.float32),
            pltpu.VMEM((16, LANES), jnp.float32),
            dma((len(operands),)),
            dma((nb,)),
            dma((nb,)),
            dma((npr,)),
            dma((npr,)),
            dma((-(-width // (2 * LANES)), nh * npr)),
            dma((-(-width // (2 * LANES)), nh * npr)),
            dma((nb * npr,)),
            dma((nb * npr,)),
            dma((npr,)),
            dma((npr,)),
        ],
        compiler_params=pltpu.CompilerParams(collective_id=0, has_side_effects=True),
    )(*operands)
    return tuple(
        pl.pallas_call(
            finish,
            out_shape=(
                jax.ShapeDtypeStruct((rows, width), jnp.bfloat16),
                jax.ShapeDtypeStruct((12, nb * rows), jnp.float32),
            ),
            in_specs=[vmem, vmem],
            out_specs=(vmem, vmem),
        )(*pieces)
    )


def solution(mesh):
    placed = (
        P(("groups", "blk"), None),
        P(("groups", "blk"), None, "pair", None),
        P(None, ("groups", "blk")),
        P(("groups", "blk")),
        P(("groups", "blk")),
        P(None, "head"),
        P(None, "head"),
        P(None, "head"),
        P(None, "head"),
        P(None, "head"),
        P("head"),
        P("head"),
        P("head", None, None),
        P(),
        P(),
    )
    return jax.shard_map(
        body,
        mesh=mesh,
        in_specs=placed,
        out_specs=(P(("groups", "blk"), None), P(None, "groups")),
        check_vma=False,
    )
```
